512 devices in a mesh: group: 2 (over core), dp: 64 (over y, z), mp: 4 (over x).
Axes of the slice: x: 4, y: 8, z: 8, core: 2. Of those that a mesh axis runs over, the one named last changes fastest.
Arguments:
- kv_up_grads: bfloat16 [65536, 4096], P(('group', 'dp'), 'mp'), may hold values from -40 to 40
- tok_grads: bfloat16 [32768, 2048], P(('group', 'dp')), may hold values from -6 to 6
- token_rows: int32 [32768], P(('group', 'dp')), may hold values from 0 to 511
- step_count: int32 [1], replicated, may hold values from 1 to 11
- master: float32 [4, 786432], P('mp', 'dp'), may hold values from -0.12 to 0.12
- moment_one: float32 [4, 786432], P('mp', 'dp'), may hold values from -0.004 to 0.004
- moment_two: float32 [4, 786432], P('mp', 'dp'), may hold values from 1e-08 to 1e-06
- average: float32 [4, 786432], P('mp', 'dp'), may hold values from -0.12 to 0.12
Outputs:
- new_kv_up: bfloat16 [512, 4096], P(None, 'mp')
- new_embed: bfloat16 [512, 2048], P('mp')
- new_master: float32 [4, 786432], P('mp', 'dp')
- new_moment_one: float32 [4, 786432], P('mp', 'dp')
- new_moment_two: float32 [4, 786432], P('mp', 'dp')
- new_average: float32 [4, 786432], P('mp', 'dp')
The draws below stay inside these ranges and needn't reach their ends.
All inputs are finite; a program needn't handle non-finite values.
Results may differ from the reference program's by a relative error of at most 0.001.
Values may be sent and summed in bfloat16 or wider, within the bound.
A program may use at most 64 MiB of HBM per device.

```python
import math
import jax
import jax.numpy as jnp
import numpy as np
from jax import lax

D = 2048
R = 512
EROWS = 512
TOKD = 256
HW = 4096
SH = 12288
TOKENS = 32768
N_GROUP = 2
N_DP = 64
N_MP = 4


SHOWN_NORM = 1.8275


def draw_kv_up_grads(key, part):
    shards = TOKENS // TOKD
    keys = jax.random.split(jax.random.fold_in(key, 17), 3)
    row_u = jax.random.uniform(keys[0], (R // 8,), jnp.float32, -1.5, 1.5)
    col_u = jax.random.uniform(keys[1], (16,), jnp.float32, -1.5, 1.5)
    row_level = jnp.repeat(jnp.exp(row_u) / SHOWN_NORM, 8)
    col_level = jnp.repeat(jnp.exp(col_u) / SHOWN_NORM, HW // 16)
    noise = jnp.clip(jax.random.normal(keys[2], (shards, R, HW), jnp.float32), -6.0, 6.0)
    value = noise * row_level[None, :, None] * col_level[None, None, :]
    return value.reshape(shards * R, HW).astype(jnp.bfloat16)


def plant(result, key, smallest, high):
    spot = [jax.random.randint(jax.random.fold_in(key, axis), (), 0, length) for axis, length in enumerate(result.shape)]
    longest = result.shape.index(max(result.shape))
    beside = spot[:longest] + [(spot[longest] + 1) % result.shape[longest]] + spot[longest + 1:]
    return result.at[tuple(spot)].set(smallest).at[tuple(beside)].set(high)


def shard_levels(key, extent, cuts, smallest, high):
    def one(position, parts):
        heights = jax.random.uniform(jax.random.fold_in(jax.random.fold_in(key, 6), position), (parts,), jnp.float32, smallest / len(cuts), high / len(cuts))
        return jnp.repeat(jnp.exp(heights), extent[position] // parts).reshape((-1,) + (1,) * (len(extent) - position - 1))

    gain = one(*cuts[0])
    for cut in cuts[1:]:
        gain = gain * one(*cut)
    return gain


def rank_bounds(number_of, lean):
    loads = [(1 << 20) // math.isqrt(rank ** lean) + 1 for rank in range(1, number_of + 1)]
    deviation = 1 + sum(loads) // (1 << 30)
    return np.cumsum(np.array([max(1, weight // deviation) for weight in loads]))


def skewed_ids(key, shape, amount, slope):
    grid = rank_bounds(amount, slope)
    lot = jax.random.randint(jax.random.fold_in(key, 1), shape, 0, int(grid[amount - 1]))
    standing = jnp.searchsorted(jnp.asarray(grid, jnp.int32), lot, side="right")
    return jax.random.permutation(jax.random.fold_in(key, 2), amount)[standing].astype(jnp.int32)


def centred(own_key, dims, scale, limit, pieces=(), dtype=jnp.bfloat16):
    level = shard_levels(own_key, dims, pieces, -0.22, 0.18) if pieces else 1.0
    drawn = jax.random.normal(own_key, dims, jnp.float32) * scale * level
    return jnp.minimum(jnp.maximum(drawn, -limit), limit).astype(dtype)


def setup_inputs(seed: int = 0) -> dict:
    key_of = jax.random.split(jax.random.key(seed), 9)
    return {
        "kv_up_grads": draw_kv_up_grads(jax.random.fold_in(key_of[8], 71), 0),
        "tok_grads": centred(key_of[1], (TOKENS, D), 1.0, 6.0, ((0, 128),)),
        "token_rows": plant(skewed_ids(key_of[2], (TOKENS,), EROWS, 2), jax.random.fold_in(key_of[2], 3), 0, EROWS - 1).astype(jnp.int32),
        "step_count": jax.random.randint(key_of[3], (1,), 1, 12).astype(jnp.int32),
        "master": centred(key_of[4], (N_MP, N_DP * SH), 0.02, 0.12, ((0, 4), (1, 64)), jnp.float32),
        "moment_one": centred(key_of[5], (N_MP, N_DP * SH), 0.0006, 0.004, ((0, 4), (1, 64)), jnp.float32),
        "moment_two": jnp.clip(jnp.exp(math.log(9.999999974752427e-07) - 4.6051702 * jax.random.uniform(key_of[6], (N_MP, N_DP * SH), jnp.float32) ** shard_levels(key_of[6], (N_MP, N_DP * SH), ((0, 4), (1, 64)), -0.2, 0.2)), 9.99999993922529e-09, 9.999999974752427e-07),
        "average": centred(key_of[7], (N_MP, N_DP * SH), 0.02, 0.12, ((0, 4), (1, 64)), jnp.float32),
    }


BETA_ONE = 0.9
BETA_TWO = 0.95
LEARN_RATE = 0.02
DECAY_RATE = 0.1
EPSILON = 1e-08
CLIP_NORM = 1.0
AVG_DECAY = 0.9

def to_state(latent, embed):
    block_cols = latent.shape[1] // N_MP
    latent_part = latent.reshape(R, N_MP, block_cols).transpose(1, 0, 2).reshape(N_MP, N_DP, -1)
    embed_part = embed.reshape(N_MP, N_DP, -1)
    return jnp.concatenate([latent_part, embed_part], axis=2).reshape(N_MP, -1)

def from_state(state):
    state_cube = state.reshape(N_MP, N_DP, -1)
    block_cols = HW // N_MP
    latent_len = R // N_DP * block_cols
    latent = state_cube[:, :, :latent_len].reshape(N_MP, R, block_cols).transpose(1, 0, 2).reshape(R, HW)
    embed = state_cube[:, :, latent_len:].reshape(EROWS, D)
    return (latent, embed)

def add_one(running, piece):
    return (running + piece.astype(jnp.float32), None)

def reference(kv_up_grads, tok_grads, token_rows, step_count, master, moment_one, moment_two, average):
    partials = kv_up_grads.reshape(N_GROUP * N_DP, R, HW)
    grad_kv, _ = lax.scan(add_one, jnp.zeros((R, HW), jnp.float32), partials)
    grad_embed = jax.ops.segment_sum(tok_grads.astype(jnp.float32), token_rows, num_segments=EROWS)
    gradient = to_state(grad_kv, grad_embed)
    norm_value = jnp.sqrt(jnp.sum(gradient * gradient))
    factor = CLIP_NORM / jnp.maximum(norm_value, CLIP_NORM)
    clipped = factor * gradient
    step_float = step_count[0].astype(jnp.float32)
    new_moment_one = BETA_ONE * moment_one + (1.0 - BETA_ONE) * clipped
    new_moment_two = BETA_TWO * moment_two + (1.0 - BETA_TWO) * clipped * clipped
    first_hat = new_moment_one / (1.0 - jnp.power(jnp.float32(BETA_ONE), step_float))
    second_hat = new_moment_two / (1.0 - jnp.power(jnp.float32(BETA_TWO), step_float))
    new_master = master - LEARN_RATE * (first_hat / (jnp.sqrt(second_hat) + EPSILON) + DECAY_RATE * master)
    new_average = AVG_DECAY * average + (1.0 - AVG_DECAY) * new_master
    new_kv_up, new_embed = from_state(new_master.astype(jnp.bfloat16))
    return (new_kv_up, new_embed, new_master, new_moment_one, new_moment_two, new_average)
```

```python
import math

import jax
import jax.numpy as jnp
import numpy as np
from jax import lax
from jax.experimental import pallas as pl
from jax.experimental.pallas import tpu as pltpu
from jax.sharding import PartitionSpec as P

BETA_ONE = 0.9
BETA_TWO = 0.95
LEARN_RATE = 0.02
DECAY_RATE = 0.1
EPSILON = 1e-08
CLIP_NORM = 1.0
AVG_DECAY = 0.9

MESH = pl.DeviceIdType.MESH
LANES = 128
ROWS = 8


def step_kernel(
    n, nx, cols, width,
    kv, tok, trow, step, master, moment_one, moment_two, average,
    okv, oem, omaster, omoment_one, omoment_two, oaverage,
    kvbuf, toks, rows, part, embuf, share, share_in, grads, state,
    norm_a, norm_b, norm_c, wem,
    state_sem, local_sem, tok_sem, kv_send, kv_recv, em_send, em_recv,
    s2_send, s2_recv, g_sem, na_send, na_recv, nb_send, nb_recv, nc_send, nc_recv,
    ga_send, ga_recv, gb_send, gb_recv, gc_send, gc_recv,
):
    group = lax.axis_index("group")
    owner = lax.axis_index("dp")
    block = lax.axis_index("mp")
    y, z = owner // n, owner % n
    other = 1 - group
    half, ehalf = cols // 2, width // 2
    chunks, echunks = half // LANES, ehalf // LANES
    one = y * other + z * group
    two = z * other + y * group

    def along_y(place):
        return place * n + z

    def along_z(place):
        return y * n + place

    def along_one(place):
        return along_y(place) * other + along_z(place) * group

    def along_two(place):
        return along_z(place) * other + along_y(place) * group

    def each(body):
        def wrapped(k, _):
            body(k)
            return 0

        lax.fori_loop(1, n, wrapped, 0)

    def remote(src, dst, send, recv, device):
        return pltpu.make_async_remote_copy(
            src_ref=src, dst_ref=dst, send_sem=send, recv_sem=recv, device_id=device, device_id_type=MESH
        )

    states = [
        pltpu.make_async_copy(ref, state.at[i], state_sem.at[i])
        for i, ref in enumerate((master, moment_one, moment_two, average))
    ]
    for copy in states:
        copy.start()

    ecols = pl.ds(pl.multiple_of(group * ehalf, ehalf), ehalf)
    ecols_other = pl.ds(pl.multiple_of(other * ehalf, ehalf), ehalf)
    tok_here = pltpu.make_async_copy(tok.at[:, ecols], toks.at[group], local_sem.at[1])
    row_here = pltpu.make_async_copy(trow, rows.at[group], local_sem.at[2])
    tok_here.start()
    row_here.start()

    barrier = pltpu.get_barrier_semaphore()

    def greet(k):
        for core in range(2):
            pl.semaphore_signal(barrier, inc=1, device_id=(core, along_y((y + k) % n), block), device_id_type=MESH)
            pl.semaphore_signal(barrier, inc=1, device_id=(core, along_z((z + k) % n), block), device_id_type=MESH)

    each(greet)
    for k in range(1, nx):
        for core in range(2):
            pl.semaphore_signal(barrier, inc=1, device_id=(core, owner, (block + k) % nx), device_id_type=MESH)
    pl.semaphore_signal(barrier, inc=1, device_id=(other, owner, block), device_id_type=MESH)
    pl.semaphore_wait(barrier, 4 * (n - 1) + 2 * (nx - 1) + 1)

    partner = (other, owner, block)
    tok_there = remote(tok.at[:, ecols_other], toks.at[group], tok_sem.at[0], tok_sem.at[1], partner)
    row_there = remote(trow, rows.at[group], tok_sem.at[2], tok_sem.at[3], partner)
    tok_there.start()
    row_there.start()

    def kv_first(place):
        return kv.at[place, :, :, pl.ds(0, half)]

    def kv_second(place):
        return kv.at[:, place, :, pl.ds(half, half)]

    def send_first(k):
        place = (y + k) % n
        return remote(kv_first(place), kvbuf.at[group, y], kv_send.at[0, k], kv_recv.at[group, y], (0, along_y(place), block))

    def send_second(k):
        place = (z + k) % n
        return remote(kv_second(place), kvbuf.at[group, z], kv_send.at[1, k], kv_recv.at[group, z], (1, along_z(place), block))

    def start_kv(k):
        send_first(k).start()
        send_second(k).start()

    keep_first = pltpu.make_async_copy(kv_first(y), kvbuf.at[group, y], local_sem.at[0])
    keep_second = pltpu.make_async_copy(kv_second(z), kvbuf.at[group, z], local_sem.at[0])
    pass_first = remote(kv_first(y), kvbuf.at[group, y], kv_send.at[0, 0], kv_recv.at[group, y], partner)
    pass_second = remote(kv_second(z), kvbuf.at[group, z], kv_send.at[0, 0], kv_recv.at[group, z], partner)

    each(start_kv)

    @pl.when(group == 0)
    def _():
        keep_first.start()
        pass_second.start()

    @pl.when(group == 1)
    def _():
        keep_second.start()
        pass_first.start()

    tok_here.wait()
    row_here.wait()
    tok_there.wait_recv()
    row_there.wait_recv()
    index = lax.broadcasted_iota(jnp.int32, (2 * n * n, 1), 0)
    first, second, pair = index // (2 * n), index % n, (index // n) % 2
    yy = first * other + second * group
    zz = second * other + first * group
    wanted = block * (2 * n * n) + 2 * (yy * n + zz) + pair
    total = jnp.zeros((2 * n * n, ehalf), jnp.float32)
    for core in range(2):
        onehot = jnp.where(wanted == rows[core], 1.0, 0.0).astype(jnp.bfloat16)
        total = total + jnp.dot(onehot, toks[core], preferred_element_type=jnp.float32)
    part[...] = total.reshape(n, 2 * n, ehalf)

    def send_em(k):
        place = (one + k) % n
        return remote(part.at[place], embuf.at[one], em_send.at[k], em_recv.at[one], (group, along_one(place), block))

    each(lambda k: send_em(k).start())
    embuf[one] = part[one]

    def wait_kv(k):
        place = (one + k) % n
        for core in range(2):
            remote(kvbuf.at[core, place], kvbuf.at[core, place], kv_send.at[0, 0], kv_recv.at[core, place], partner).wait_recv()

    each(wait_kv)
    remote(kvbuf.at[other, one], kvbuf.at[other, one], kv_send.at[0, 0], kv_recv.at[other, one], partner).wait_recv()
    keep_first.wait()

    def wait_em(k):
        place = (one + k) % n
        remote(part.at[0], embuf.at[place], em_send.at[0], em_recv.at[place], partner).wait_recv()

    each(wait_em)

    for c in range(echunks):
        span = pl.ds(c * LANES, LANES)
        for i in range(2):
            piece = embuf[0, pl.ds(i * n, n), span]
            for place in range(1, n):
                piece = piece + embuf[place, pl.ds(i * n, n), span]
            share[chunks + i, pl.ds(c, n, stride=ROWS), :] = piece

    def sum_kv(place):
        at = pl.ds(pl.multiple_of(place * ROWS, ROWS), ROWS)
        for c in range(chunks):
            span = pl.ds(c * LANES, LANES)
            acc = jnp.zeros((ROWS, LANES), jnp.float32)
            for core in range(2):
                for source in range(n):
                    acc = acc + kvbuf[core, source, place, :, span].astype(jnp.float32)
            share[c, at, :] = acc

    def send_share(k):
        place = (two + k) % n
        return remote(
            share.at[:, pl.ds(pl.multiple_of(place * ROWS, ROWS), ROWS), :],
            share_in.at[two], s2_send.at[k], s2_recv.at[two], (group, along_two(place), block),
        )

    def sum_and_send(k):
        sum_kv((two + k) % n)
        send_share(k).start()

    each(sum_and_send)
    sum_kv(two)
    share_in[two] = share[:, pl.ds(pl.multiple_of(two * ROWS, ROWS), ROWS), :]

    def wait_share(k):
        place = (two + k) % n
        remote(share_in.at[place], share_in.at[place], s2_send.at[0], s2_recv.at[place], partner).wait_recv()

    each(wait_share)
    mine = share_in[0]
    for place in range(1, n):
        mine = mine + share_in[place]
    grads[group] = mine
    swap = remote(grads.at[group], grads.at[group], g_sem.at[0], g_sem.at[1], partner)
    swap.start()

    squares = mine * mine
    lanes = squares[0]
    for c in range(1, chunks + 2):
        lanes = lanes + squares[c]
    norm_a[y] = jnp.sum(lanes, axis=0, keepdims=True)

    def send_a(k):
        place = (y + k) % n
        return remote(norm_a.at[y], norm_a.at[y], na_send.at[k], na_recv.at[y], (group, along_y(place), block))

    def wait_a(k):
        place = (y + k) % n
        remote(norm_a.at[place], norm_a.at[place], na_send.at[0], na_recv.at[place], partner).wait_recv()

    each(lambda k: send_a(k).start())
    each(wait_a)
    partial = norm_a[0]
    for place in range(1, n):
        partial = partial + norm_a[place]
    norm_b[z] = partial

    def send_b(k):
        place = (z + k) % n
        return remote(norm_b.at[z], norm_b.at[z], nb_send.at[k], nb_recv.at[z], (group, along_z(place), block))

    def wait_b(k):
        place = (z + k) % n
        remote(norm_b.at[place], norm_b.at[place], nb_send.at[0], nb_recv.at[place], partner).wait_recv()

    each(lambda k: send_b(k).start())
    each(wait_b)
    partial = norm_b[0]
    for place in range(1, n):
        partial = partial + norm_b[place]
    norm_c[group, block] = partial

    def send_c(k, core):
        place = (block + k) % nx
        to = group if core == 0 else other
        slot = 2 * k + core
        return remote(
            norm_c.at[group, block], norm_c.at[group, block], nc_send.at[slot], nc_recv.at[group, block], (to, owner, place)
        )

    fan = [(k, core) for k in range(nx) for core in range(2) if k or core]
    for k, core in fan:
        send_c(k, core).start()
    for k, core in fan:
        place = (block + k) % nx
        source = group if core == 0 else other
        remote(
            norm_c.at[source, place], norm_c.at[source, place], nc_send.at[0], nc_recv.at[source, place], partner
        ).wait_recv()
    partial = jnp.zeros((1, LANES), jnp.float32)
    for core in range(2):
        for place in range(nx):
            partial = partial + norm_c[core, place]
    norm_value = jnp.sqrt(jnp.sum(partial, axis=1, keepdims=True))
    factor = CLIP_NORM / jnp.maximum(norm_value, CLIP_NORM)

    swap.wait_recv()
    for copy in states:
        copy.wait()

    step_float = jnp.full((1, LANES), step[0], jnp.int32).astype(jnp.float32)
    one_scale = 1.0 - jnp.exp(step_float * math.log(np.float32(BETA_ONE)))
    two_scale = 1.0 - jnp.exp(step_float * math.log(np.float32(BETA_TWO)))

    def update(at, gradient):
        clipped = factor * gradient
        weight = state[0, at, :]
        new_one = BETA_ONE * state[1, at, :] + (1.0 - BETA_ONE) * clipped
        new_two = BETA_TWO * state[2, at, :] + (1.0 - BETA_TWO) * clipped * clipped
        first_hat = new_one / one_scale
        second_hat = new_two / two_scale
        new_weight = weight - LEARN_RATE * (first_hat / (jnp.sqrt(second_hat) + EPSILON) + DECAY_RATE * weight)
        omaster[at, :] = new_weight
        omoment_one[at, :] = new_one
        omoment_two[at, :] = new_two
        oaverage[at, :] = AVG_DECAY * state[3, at, :] + (1.0 - AVG_DECAY) * new_weight
        return new_weight

    row_chunks = cols // LANES
    for h in range(2):
        for c in range(chunks):
            span = pl.ds(h * half + c * LANES, LANES)
            new = update(pl.ds(h * chunks + c, ROWS, stride=row_chunks), grads[h, c])

            @pl.when(group == h)
            def _(new=new, span=span):
                okv[y, z, :, span] = new.astype(jnp.bfloat16)

        for i in range(2):
            at = pl.ds(ROWS * row_chunks + (i * 2 + h) * echunks, echunks)
            wem[h, pl.ds(i * echunks, echunks), :] = update(at, grads[h, chunks + i, 0:echunks, :])

    for c in range(echunks):
        for h in range(2):
            @pl.when(group == h)
            def _(h=h, c=c):
                oem[y, z, :, pl.ds(h * ehalf + c * LANES, LANES)] = wem[h, pl.ds(c, 2, stride=echunks), :].astype(jnp.bfloat16)

    kcols = pl.ds(pl.multiple_of(group * half, half), half)

    def gather_one(ref, span, kind, k):
        place = (one + k) % n
        here = ref.at[y, z, :, span]
        return remote(here, here, ga_send.at[kind, k], ga_recv.at[kind, one], (group, along_one(place), block))

    def send_ga(k):
        gather_one(okv, kcols, 0, k).start()
        gather_one(oem, ecols, 1, k).start()

    each(send_ga)

    def wait_ga(k):
        place = (one + k) % n
        for kind, ref, span in ((0, okv, kcols), (1, oem, ecols)):
            here = ref.at[y, z, :, span]
            remote(here, here, ga_send.at[kind, 0], ga_recv.at[kind, place], partner).wait_recv()

    each(wait_ga)

    def line(ref, core, place):
        if core == 0:
            return ref.at[:, place, :, pl.ds(0, ref.shape[3] // 2)]
        return ref.at[place, :, :, pl.ds(ref.shape[3] // 2, ref.shape[3] // 2)]

    def gather_two(core, kind, ref, k):
        place = (two + k) % n
        here = line(ref, core, two)
        return remote(here, here, gb_send.at[kind, k], gb_recv.at[kind, two], (core, along_two(place), block))

    def hand_over(core, kind, ref, place):
        here = line(ref, core, place)
        return remote(here, here, gc_send.at[kind, place], gc_recv.at[kind, place], partner)

    for core in range(2):
        @pl.when(group == core)
        def _(core=core):
            outs = ((0, okv), (1, oem))

            def send_gb(k):
                for kind, ref in outs:
                    gather_two(core, kind, ref, k).start()

            each(send_gb)
            for kind, ref in outs:
                hand_over(core, kind, ref, two).start()

            def pass_on(k):
                place = (two + k) % n
                for kind, ref in outs:
                    here = line(ref, core, place)
                    remote(here, here, gb_send.at[kind, 0], gb_recv.at[kind, place], partner).wait_recv()
                    hand_over(core, kind, ref, place).start()

            each(pass_on)

            def finish(place, _):
                for kind, ref in outs:
                    hand_over(1 - core, kind, ref, place).wait_recv()
                    hand_over(core, kind, ref, place).wait_send()
                return 0

            lax.fori_loop(0, n, finish, 0)

            def sent_gb(k):
                for kind, ref in outs:
                    gather_two(core, kind, ref, k).wait_send()

            each(sent_gb)

    tok_there.wait_send()
    row_there.wait_send()
    pass_first.wait_send()
    swap.wait_send()

    def sent(k):
        send_first(k).wait_send()
        send_second(k).wait_send()
        send_em(k).wait_send()
        send_share(k).wait_send()
        send_a(k).wait_send()
        send_b(k).wait_send()
        gather_one(okv, kcols, 0, k).wait_send()
        gather_one(oem, ecols, 1, k).wait_send()

    each(sent)
    for k, core in fan:
        send_c(k, core).wait_send()


def solution(mesh):
    owners, blocks = mesh.shape["dp"], mesh.shape["mp"]
    n = math.isqrt(owners)

    def shards(kv_up_grads, tok_grads, token_rows, step_count, master, moment_one, moment_two, average):
        cols, width, tokens = kv_up_grads.shape[1], tok_grads.shape[1], tok_grads.shape[0]
        rows = master.shape[1] // LANES
        half, ehalf = cols // 2, width // 2
        lines = lambda array: array.reshape(rows, LANES)
        dma, f32, bf16 = pltpu.SemaphoreType.DMA, jnp.float32, jnp.bfloat16
        any_space = pl.BlockSpec(memory_space=pltpu.HBM)
        vmem = pl.BlockSpec(memory_space=pltpu.VMEM)
        state = jax.ShapeDtypeStruct((rows, LANES), f32)
        share = half // LANES + 2

        def body(*refs):
            step_kernel(n, blocks, cols, width, *refs)

        outs = pl.pallas_call(
            body,
            out_shape=(
                jax.ShapeDtypeStruct((n, n, ROWS, cols), bf16),
                jax.ShapeDtypeStruct((n, n, 2, width), bf16),
                state, state, state, state,
            ),
            in_specs=[any_space] * 3 + [pl.BlockSpec(memory_space=pltpu.SMEM)] + [any_space] * 4,
            out_specs=[vmem] * 6,
            scratch_shapes=[
                pltpu.VMEM((2, n, n, ROWS, half), bf16),
                pltpu.VMEM((2, tokens, ehalf), bf16),
                pltpu.VMEM((2, 1, tokens), jnp.int32),
                pltpu.VMEM((n, 2 * n, ehalf), f32),
                pltpu.VMEM((n, 2 * n, ehalf), f32),
                pltpu.VMEM((share, n * ROWS, LANES), f32),
                pltpu.VMEM((n, share, ROWS, LANES), f32),
                pltpu.VMEM((2, share, ROWS, LANES), f32),
                pltpu.VMEM((4, rows, LANES), f32),
                pltpu.VMEM((n, 1, LANES), f32),
                pltpu.VMEM((n, 1, LANES), f32),
                pltpu.VMEM((2, blocks, 1, LANES), f32),
                pltpu.VMEM((2, 2 * (ehalf // LANES), LANES), f32),
                dma((4,)), dma((3,)), dma((4,)),
                dma((2, n)), dma((2, n)), dma((n,)), dma((n,)),
                dma((n,)), dma((n,)), dma((2,)),
                dma((n,)), dma((n,)), dma((n,)), dma((n,)),
                dma((2 * blocks,)), dma((2, blocks)),
                dma((2, n)), dma((2, n)), dma((2, n)), dma((2, n)), dma((2, n)), dma((2, n)),
            ],
            compiler_params=pltpu.CompilerParams(
                collective_id=0, has_side_effects=True, vmem_limit_bytes=48 * 1024 * 1024
            ),
            name="adam_step",
        )(
            kv_up_grads.reshape(n, n, ROWS, cols), tok_grads, token_rows.reshape(1, tokens), step_count,
            lines(master), lines(moment_one), lines(moment_two), lines(average),
        )
        new_kv_up, new_embed, *states = outs
        return (
            new_kv_up.reshape(owners * ROWS, cols),
            new_embed.reshape(owners * 2, width),
            *[array.reshape(1, rows * LANES) for array in states],
        )

    placed = (
        P(("group", "dp"), "mp"),
        P(("group", "dp"), None),
        P(("group", "dp")),
        P(),
        P("mp", "dp"),
        P("mp", "dp"),
        P("mp", "dp"),
        P("mp", "dp"),
    )
    return jax.shard_map(
        shards,
        mesh=mesh,
        in_specs=placed,
        out_specs=(
            P(None, "mp"),
            P("mp", None),
            P("mp", "dp"),
            P("mp", "dp"),
            P("mp", "dp"),
            P("mp", "dp"),
        ),
        check_vma=False,
    )
```

```python
import math

import jax
import jax.numpy as jnp
import numpy as np
from jax import lax
from jax.experimental import pallas as pl
from jax.experimental.pallas import tpu as pltpu
from jax.sharding import PartitionSpec as P

BETA_ONE = 0.9
BETA_TWO = 0.95
LEARN_RATE = 0.02
DECAY_RATE = 0.1
EPSILON = 1e-08
CLIP_NORM = 1.0
AVG_DECAY = 0.9

MESH = pl.DeviceIdType.MESH
LANES = 128
ROWS = 8


def step_kernel(
    n, nx, cols, width,
    kv, tok, trow, step, master, moment_one, moment_two, average,
    okv, oem, omaster, omoment_one, omoment_two, oaverage,
    near, far, farh, hop, hop_in, toks, rows, part, enear, efar, efarh, ehop, ehop_in,
    share, share_in, grads, state, fresh, norm_a, norm_b, norm_c, wem, gkv, gem,
    state_sem, fresh_sem, tok_sem, kv_send, near_recv, far_recv, farh_recv, hop_send, hop_recv,
    em_send, enear_recv, efar_recv, efarh_recv, ehop_send, ehop_recv,
    s2_send, s2_recv, g_sem, na_send, na_recv, nb_send, nb_recv, nc_send, nc_recv,
    ga_send, ga_recv, gb_send, gb_near, gb_two, gb_fwd, gb_third, gb_four,
    ge_send, ge_near, ge_two, ge_fwd, ge_third, ge_four, gc_send, gc_recv, out_sem,
):
    group = lax.axis_index("group")
    owner = lax.axis_index("dp")
    block = lax.axis_index("mp")
    y, z = owner // n, owner % n
    other = 1 - group
    half, ehalf = cols // 2, width // 2
    chunks, echunks = half // LANES, ehalf // LANES
    one = y * other + z * group
    two = z * other + y * group
    sides = ((0, 1), (1, n - 1))

    def along_y(place):
        return place * n + z

    def along_z(place):
        return y * n + place

    def along_one(place):
        return along_y(place) * other + along_z(place) * group

    def along_two(place):
        return along_z(place) * other + along_y(place) * group

    def each(body):
        def wrapped(k, _):
            body(k)
            return 0

        lax.fori_loop(1, n, wrapped, 0)

    def near_first(i):
        return (i // 2 + 1) * (1 - i % 2) + (n - 1 - i // 2) * (i % 2)

    def in_order(body):
        def wrapped(i, _):
            body(near_first(i))
            return 0

        lax.fori_loop(0, n - 1, wrapped, 0)

    def far_first(body):
        def wrapped(i, _):
            body(near_first(n - 2 - i))
            return 0

        lax.fori_loop(0, n - 1, wrapped, 0)

    def remote(src, dst, send, recv, device):
        return pltpu.make_async_remote_copy(
            src_ref=src, dst_ref=dst, send_sem=send, recv_sem=recv, device_id=device, device_id_type=MESH
        )

    partner = (other, owner, block)

    def arrive(dst, recv):
        remote(dst, dst, g_sem.at[0], recv, partner).wait_recv()

    def land(dst, sem):
        pltpu.make_async_copy(dst, dst, sem).wait()

    states = [
        pltpu.make_async_copy(ref, state.at[i], state_sem.at[i])
        for i, ref in enumerate((master, moment_one, moment_two, average))
    ]
    ecols = pl.ds(pl.multiple_of(group * ehalf, ehalf), ehalf)
    ecols_other = pl.ds(pl.multiple_of(other * ehalf, ehalf), ehalf)
    tok_here = pltpu.make_async_copy(tok.at[:, ecols], toks.at[group], tok_sem.at[4])
    row_here = pltpu.make_async_copy(trow, rows.at[group], tok_sem.at[5])
    tok_here.start()
    row_here.start()

    barrier = pltpu.get_barrier_semaphore()

    def greet(k):
        pl.semaphore_signal(barrier, inc=1, device_id=(group, along_one((one + k) % n), block), device_id_type=MESH)
        pl.semaphore_signal(barrier, inc=1, device_id=(group, along_two((two + k) % n), block), device_id_type=MESH)

    far_first(greet)
    for k in (2, n - 2, 1, n - 1):
        pl.semaphore_signal(barrier, inc=1, device_id=(other, along_one((one + k) % n), block), device_id_type=MESH)
    for k in range(1, nx):
        for core in range(2):
            pl.semaphore_signal(barrier, inc=1, device_id=(core, owner, (block + k) % nx), device_id_type=MESH)
    pl.semaphore_signal(barrier, inc=1, device_id=partner, device_id_type=MESH)
    pl.semaphore_wait(barrier, 2 * (n - 1) + 4 + 2 * (nx - 1) + 1)

    def kv_share(h, place):
        if h == 0:
            return kv.at[place, :, :, pl.ds(0, half)]
        return kv.at[:, place, :, pl.ds(half, half)]

    def kv_part(h, place, side):
        if h == 0:
            return kv.at[place, pl.ds(side * (n // 2), n // 2), :, pl.ds(0, half)]
        return kv.at[pl.ds(side * (n // 2), n // 2), place, :, pl.ds(half, half)]

    here = (y, z)
    away = (lambda place: (0, along_y(place), block), lambda place: (1, along_z(place), block))
    out = []
    for h in range(2):
        at = here[h]
        for side, sign in sides:
            out.append(remote(
                kv_part(h, (at + 4) % n, side), farh.at[side, group],
                kv_send.at[h, side], farh_recv.at[side, group], away[h]((at + 2 * sign) % n),
            ))
    for h in range(2):
        at = here[h]
        for side, sign in sides:
            out.append(remote(
                kv_share(h, (at + 3 * sign) % n), far.at[side, group, 1],
                kv_send.at[h, 2 + side], far_recv.at[side, group, 1], away[h]((at + sign) % n),
            ))
    for copy in out:
        copy.start()
    for h in range(2):
        at = here[h]
        kept = [(far.at[side, group, 0], far_recv.at[side, group, 0], (at + 2 * sign) % n) for side, sign in sides]
        kept.append((near.at[group, 0], near_recv.at[group, 0], at))

        @pl.when(group == h)
        def _(h=h, kept=kept):
            for dst, sem, place in kept:
                pltpu.make_async_copy(kv_share(h, place), dst, sem).start()

        @pl.when(group != h)
        def _(h=h, kept=kept):
            for i, (dst, sem, place) in enumerate(kept):
                remote(kv_share(h, place), dst, kv_send.at[2, i], sem, partner).start()

    tok_there = remote(tok.at[:, ecols_other], toks.at[group], tok_sem.at[0], tok_sem.at[1], partner)
    row_there = remote(trow, rows.at[group], tok_sem.at[2], tok_sem.at[3], partner)
    tok_there.start()
    row_there.start()
    for h in range(2):
        at = here[h]
        for side, sign in sides:
            copy = remote(
                kv_share(h, (at + sign) % n), near.at[group, 1 + side],
                kv_send.at[h, 4 + side], near_recv.at[group, 1 + side], away[h]((at + sign) % n),
            )
            copy.start()
            out.append(copy)
    for copy in states:
        copy.start()

    tok_here.wait()
    row_here.wait()
    tok_there.wait_recv()
    row_there.wait_recv()
    index = lax.broadcasted_iota(jnp.int32, (2 * n * n, 1), 0)
    first, second, pair = index // (2 * n), index % n, (index // n) % 2
    yy = first * other + second * group
    zz = second * other + first * group
    wanted = block * (2 * n * n) + 2 * (yy * n + zz) + pair
    total = jnp.zeros((2 * n * n, ehalf), jnp.float32)
    for core in range(2):
        onehot = jnp.where(wanted == rows[core], 1.0, 0.0).astype(jnp.bfloat16)
        total = total + jnp.dot(onehot, toks[core], preferred_element_type=jnp.float32)
    part[...] = total.reshape(n, 2 * n, ehalf)

    def ring(place):
        return (group, along_one(place % n), block)

    eout = []
    for side, sign in sides:
        eout.append(remote(
            part.at[(one + 4) % n, pl.ds(side * n, n)], efarh.at[side],
            em_send.at[0, side], efarh_recv.at[side], ring(one + 2 * sign),
        ))
    for side, sign in sides:
        eout.append(remote(
            part.at[(one + 3 * sign) % n], efar.at[side], em_send.at[1, side], efar_recv.at[side], ring(one + sign),
        ))
    for side, sign in sides:
        eout.append(remote(
            part.at[(one + sign) % n], enear.at[side], em_send.at[2, side], enear_recv.at[side], ring(one + sign),
        ))
    for copy in eout:
        copy.start()

    hops, ehops = [], []
    for side, sign in sides:
        land(far.at[side, group, 0], far_recv.at[side, group, 0])
        arrive(far.at[side, other, 0], far_recv.at[side, other, 0])
        for core in range(2):
            arrive(far.at[side, core, 1], far_recv.at[side, core, 1])
            arrive(farh.at[side, core], farh_recv.at[side, core])
        low = side * (n // 2)

        def add_four(row, _, side=side):
            for c in range(chunks):
                span = pl.ds(c * LANES, LANES)
                acc = far[side, 0, 0, row, :, span].astype(jnp.float32)
                for core, source in ((1, 0), (0, 1), (1, 1)):
                    acc = acc + far[side, core, source, row, :, span].astype(jnp.float32)
                hop[side, row, :, span] = acc
            return 0

        def add_six(i, _, side=side, low=low):
            row = low + i
            for c in range(chunks):
                span = pl.ds(c * LANES, LANES)
                acc = far[side, 0, 0, row, :, span].astype(jnp.float32)
                for core, source in ((1, 0), (0, 1), (1, 1)):
                    acc = acc + far[side, core, source, row, :, span].astype(jnp.float32)
                for core in range(2):
                    acc = acc + farh[side, core, i, :, span].astype(jnp.float32)
                hop[side, row, :, span] = acc
            return 0

        lax.fori_loop(n // 2 - low, n - low, add_four, 0)
        lax.fori_loop(0, n // 2, add_six, 0)
        copy = remote(hop.at[side], hop_in.at[side], hop_send.at[side], hop_recv.at[side], ring(one + 2 * sign))
        copy.start()
        hops.append(copy)

    for side, sign in sides:
        arrive(efar.at[side], efar_recv.at[side])
        arrive(efarh.at[side], efarh_recv.at[side])
        to = (one + 2 * sign) % n
        for i in range(2):
            at = pl.ds(i * n, n)
            if i == side:
                ehop[side, at, :] = part[to, at, :] + efar[side, at, :] + efarh[side]
            else:
                ehop[side, at, :] = part[to, at, :] + efar[side, at, :]
        copy = remote(ehop.at[side], ehop_in.at[side], ehop_send.at[side], ehop_recv.at[side], ring(one + 2 * sign))
        copy.start()
        ehops.append(copy)

    land(near.at[group, 0], near_recv.at[group, 0])
    arrive(near.at[other, 0], near_recv.at[other, 0])
    for core in range(2):
        for side in range(2):
            arrive(near.at[core, 1 + side], near_recv.at[core, 1 + side])

    def add_near(row, _):
        at = pl.ds(pl.multiple_of(row * ROWS, ROWS), ROWS)
        for c in range(chunks):
            span = pl.ds(c * LANES, LANES)
            acc = near[0, 0, row, :, span].astype(jnp.float32)
            for core, source in ((1, 0), (0, 1), (1, 1), (0, 2), (1, 2)):
                acc = acc + near[core, source, row, :, span].astype(jnp.float32)
            share[c, at, :] = acc
        return 0

    lax.fori_loop(0, n, add_near, 0)
    for side in range(2):
        arrive(enear.at[side], enear_recv.at[side])
    enear[0] = part[one] + enear[0] + enear[1]
    for side in range(2):
        arrive(hop_in.at[side], hop_recv.at[side])

    def add_hops(row, _):
        at = pl.ds(pl.multiple_of(row * ROWS, ROWS), ROWS)
        for c in range(chunks):
            span = pl.ds(c * LANES, LANES)
            share[c, at, :] = share[c, at, :] + hop_in[0, row, :, span] + hop_in[1, row, :, span]
        return 0

    lax.fori_loop(0, n, add_hops, 0)
    for side in range(2):
        arrive(ehop_in.at[side], ehop_recv.at[side])
    for c in range(echunks):
        span = pl.ds(c * LANES, LANES)
        for i in range(2):
            at = pl.ds(i * n, n)
            piece = enear[0, at, span] + ehop_in[0, at, span] + ehop_in[1, at, span]
            share[chunks + i, pl.ds(c, n, stride=ROWS), :] = piece

    def send_share(k):
        place = (two + k) % n
        return remote(
            share.at[:, pl.ds(pl.multiple_of(place * ROWS, ROWS), ROWS), :],
            share_in.at[two], s2_send.at[k], s2_recv.at[two], (group, along_two(place), block),
        )

    far_first(lambda k: send_share(k).start())
    share_in[two] = share[:, pl.ds(pl.multiple_of(two * ROWS, ROWS), ROWS), :]

    def wait_share(k):
        place = (two + k) % n
        arrive(share_in.at[place], s2_recv.at[place])

    in_order(wait_share)
    mine = share_in[0]
    for place in range(1, n):
        mine = mine + share_in[place]
    grads[group] = mine
    swap = remote(grads.at[group], grads.at[group], g_sem.at[0], g_sem.at[1], partner)
    swap.start()

    squares = mine * mine
    lanes = squares[0]
    for c in range(1, chunks + 2):
        lanes = lanes + squares[c]
    norm_a[y] = jnp.sum(lanes, axis=0, keepdims=True)

    def send_a(k):
        place = (y + k) % n
        return remote(norm_a.at[y], norm_a.at[y], na_send.at[k], na_recv.at[y], (group, along_y(place), block))

    def wait_a(k):
        place = (y + k) % n
        arrive(norm_a.at[place], na_recv.at[place])

    far_first(lambda k: send_a(k).start())
    in_order(wait_a)
    partial = norm_a[0]
    for place in range(1, n):
        partial = partial + norm_a[place]
    norm_b[z] = partial

    def send_b(k):
        place = (z + k) % n
        return remote(norm_b.at[z], norm_b.at[z], nb_send.at[k], nb_recv.at[z], (group, along_z(place), block))

    def wait_b(k):
        place = (z + k) % n
        arrive(norm_b.at[place], nb_recv.at[place])

    far_first(lambda k: send_b(k).start())
    in_order(wait_b)
    partial = norm_b[0]
    for place in range(1, n):
        partial = partial + norm_b[place]
    norm_c[group, block] = partial

    def send_c(k, core):
        place = (block + k) % nx
        to = group if core == 0 else other
        slot = 2 * k + core
        return remote(
            norm_c.at[group, block], norm_c.at[group, block], nc_send.at[slot], nc_recv.at[group, block], (to, owner, place)
        )

    fan = [(k, core) for k in range(nx) for core in range(2) if k or core]
    for k, core in fan:
        send_c(k, core).start()
    for k, core in fan:
        place = (block + k) % nx
        source = group if core == 0 else other
        arrive(norm_c.at[source, place], nc_recv.at[source, place])
    partial = jnp.zeros((1, LANES), jnp.float32)
    for core in range(2):
        for place in range(nx):
            partial = partial + norm_c[core, place]
    norm_value = jnp.sqrt(jnp.sum(partial, axis=1, keepdims=True))
    factor = CLIP_NORM / jnp.maximum(norm_value, CLIP_NORM)

    swap.wait_recv()
    for copy in states:
        copy.wait()

    step_float = jnp.full((1, LANES), step[0], jnp.int32).astype(jnp.float32)
    one_scale = 1.0 - jnp.exp(step_float * math.log(np.float32(BETA_ONE)))
    two_scale = 1.0 - jnp.exp(step_float * math.log(np.float32(BETA_TWO)))

    def update(at, gradient):
        clipped = factor * gradient
        weight = state[0, at, :]
        new_one = BETA_ONE * state[1, at, :] + (1.0 - BETA_ONE) * clipped
        new_two = BETA_TWO * state[2, at, :] + (1.0 - BETA_TWO) * clipped * clipped
        first_hat = new_one / one_scale
        second_hat = new_two / two_scale
        new_weight = weight - LEARN_RATE * (first_hat / (jnp.sqrt(second_hat) + EPSILON) + DECAY_RATE * weight)
        fresh[0, at, :] = new_weight
        fresh[1, at, :] = new_one
        fresh[2, at, :] = new_two
        fresh[3, at, :] = AVG_DECAY * state[3, at, :] + (1.0 - AVG_DECAY) * new_weight
        return new_weight

    row_chunks = cols // LANES
    for h in range(2):
        for c in range(chunks):
            span = pl.ds(h * half + c * LANES, LANES)
            new = update(pl.ds(h * chunks + c, ROWS, stride=row_chunks), grads[h, c])

            @pl.when(group == h)
            def _(new=new, span=span):
                gkv[y, z, :, span] = new.astype(jnp.bfloat16)

        for i in range(2):
            at = pl.ds(ROWS * row_chunks + (i * 2 + h) * echunks, echunks)
            wem[h, pl.ds(i * echunks, echunks), :] = update(at, grads[h, chunks + i, 0:echunks, :])

    for c in range(echunks):
        for h in range(2):
            @pl.when(group == h)
            def _(h=h, c=c):
                gem[y, z, :, pl.ds(h * ehalf + c * LANES, LANES)] = wem[h, pl.ds(c, 2, stride=echunks), :].astype(jnp.bfloat16)

    kcols = pl.ds(pl.multiple_of(group * half, half), half)

    def block_of(ref, place_one, place_two, span):
        return ref.at[place_one * other + place_two * group, place_two * other + place_one * group, :, span]

    def gather_one(ref, span, kind, k):
        place = (one + k) % n
        mine = block_of(ref, one, two, span)
        return remote(mine, mine, ga_send.at[kind, k], ga_recv.at[kind, one], (group, along_one(place), block))

    def came_one(ref, span, kind, place):
        arrive(block_of(ref, place, two, span), ga_recv.at[kind, place])

    def second(place):
        return (group, along_two(place % n), block)

    def spread(place):
        ref = block_of(gkv, place, two, kcols)
        for side, sign in sides:
            remote(ref, ref, gb_send.at[1, side], gb_two.at[side, place], second(two + 2 * sign)).start()
        for side, sign in sides:
            remote(ref, ref, gb_send.at[0, side], gb_near.at[side], second(two + sign)).start()

    def half_cols(side):
        return pl.ds(pl.multiple_of(group * half + side * (half // 2), half // 2), half // 2)

    def forward(place):
        for side, sign in sides:
            source = (two - 2 * sign + 2 * n) % n
            ref = block_of(gkv, place, source, kcols)
            arrive(ref, gb_two.at[side, place])
            remote(ref, ref, gb_fwd.at[0, side], gb_third.at[side], second(two + sign)).start()
            ref = block_of(gkv, place, source, half_cols(side))
            remote(ref, ref, gb_fwd.at[1, side], gb_four.at[side], second(two + 2 * sign)).start()

    def line(ref, core, place, side=None):
        wide = ref.shape[3] // 2
        span = pl.ds(core * wide, wide) if side is None else pl.ds(core * wide + side * (wide // 2), wide // 2)
        return ref.at[:, place, :, span] if core == 0 else ref.at[place, :, :, span]

    far_first(lambda k: gather_one(gkv, kcols, 0, k).start())
    far_first(lambda k: gather_one(gem, ecols, 1, k).start())
    spread(one)

    def relay(k):
        place = (one + k) % n
        came_one(gkv, kcols, 0, place)
        spread(place)

    in_order(relay)
    in_order(lambda k: came_one(gem, ecols, 1, (one + k) % n))

    results = ((0, gkv, okv), (1, gem, oem))
    for i, ref in enumerate((omaster, omoment_one, omoment_two, oaverage)):
        pltpu.make_async_copy(fresh.at[i], ref, fresh_sem.at[i]).start()

    for core in range(2):
        @pl.when(group == core)
        def _(core=core):
            def hand_over(place):
                for kind, ref, result in results:
                    mine = line(ref, core, place)
                    remote(mine, mine, gc_send.at[kind, place], gc_recv.at[kind, place], partner).start()
                    pltpu.make_async_copy(mine, line(result, core, place), out_sem.at[core, kind, place]).start()

            mine = line(gem, core, two)
            for side, sign in sides:
                remote(mine, mine, ge_send.at[1, side], ge_two.at[side], second(two + 2 * sign)).start()
            for side, sign in sides:
                remote(mine, mine, ge_send.at[0, side], ge_near.at[side], second(two + sign)).start()
            hand_over(two)
            forward(one)
            in_order(lambda k: forward((one + k) % n))
            for side, sign in sides:
                source = (two - 2 * sign + 2 * n) % n
                ref = line(gem, core, source)
                arrive(ref, ge_two.at[side])
                remote(ref, ref, ge_fwd.at[0, side], ge_third.at[side], second(two + sign)).start()
                ref = line(gem, core, source, side)
                remote(ref, ref, ge_fwd.at[1, side], ge_four.at[side], second(two + 2 * sign)).start()
            for side, sign in sides:
                source = (two - sign + n) % n
                arrive(line(gkv, core, source), gb_near.at[side])
                arrive(line(gem, core, source), ge_near.at[side])
                hand_over(source)
            for side, sign in sides:
                hand_over((two - 2 * sign + 2 * n) % n)
            for side, sign in sides:
                source = (two - 3 * sign + 3 * n) % n
                arrive(line(gkv, core, source), gb_third.at[side])
                arrive(line(gem, core, source), ge_third.at[side])
                hand_over(source)
            source = (two + 4) % n
            for side, sign in sides:
                arrive(line(gkv, core, source, side), gb_four.at[side])
                arrive(line(gem, core, source, side), ge_four.at[side])
            hand_over(source)

            def take(place, _):
                for kind, ref, result in results:
                    theirs = line(ref, 1 - core, place)
                    arrive(theirs, gc_recv.at[kind, place])
                    pltpu.make_async_copy(theirs, line(result, 1 - core, place), out_sem.at[1 - core, kind, place]).start()
                return 0

            lax.fori_loop(0, n, take, 0)

            def sent_lines(place, _):
                for kind, ref, result in results:
                    mine = line(ref, core, place)
                    remote(mine, mine, gc_send.at[kind, place], gc_recv.at[kind, place], partner).wait_send()
                    for h in range(2):
                        pltpu.make_async_copy(line(ref, h, place), line(result, h, place), out_sem.at[h, kind, place]).wait()
                return 0

            lax.fori_loop(0, n, sent_lines, 0)
            for side in range(2):
                for i in range(2):
                    for ref, sends in ((gkv, gb_send), (gem, ge_send)):
                        mine = line(ref, core, two)
                        remote(mine, mine, sends.at[i, side], g_sem.at[1], partner).wait_send()
                for ref, sends in ((gkv, gb_fwd), (gem, ge_fwd)):
                    mine = line(ref, core, two)
                    remote(mine, mine, sends.at[0, side], g_sem.at[1], partner).wait_send()
                    mine = line(ref, core, two, side)
                    remote(mine, mine, sends.at[1, side], g_sem.at[1], partner).wait_send()

    for copy in out + eout + hops + ehops:
        copy.wait_send()
    for i in range(3):
        remote(near.at[0, 0], near.at[0, 0], kv_send.at[2, i], g_sem.at[1], partner).wait_send()
    tok_there.wait_send()
    row_there.wait_send()
    swap.wait_send()

    def sent(k):
        send_share(k).wait_send()
        send_a(k).wait_send()
        send_b(k).wait_send()
        gather_one(gkv, kcols, 0, k).wait_send()
        gather_one(gem, ecols, 1, k).wait_send()

    each(sent)
    for k, core in fan:
        send_c(k, core).wait_send()
    for i, ref in enumerate((omaster, omoment_one, omoment_two, oaverage)):
        pltpu.make_async_copy(fresh.at[i], ref, fresh_sem.at[i]).wait()


def write_out(kv, em, *refs):
    states, (okv, oem), out_states = refs[:4], refs[4:6], refs[6:10]
    kv_in, em_in, em_out, state_in, read, write = refs[10:]
    pieces = kv_in.shape[0]
    cut = kv.shape[0] // pieces
    plan = [(kv.at[pl.ds(i * cut, cut)], kv_in.at[i], okv.at[pl.ds(i * cut, cut)]) for i in range(pieces)]
    plan += [(states[i], state_in.at[i], out_states[i]) for i in range(4)]
    plan += [(em, em_in, None)]
    reads = [pltpu.make_async_copy(src, mid, read.at[i]) for i, (src, mid, _) in enumerate(plan)]
    for copy in reads:
        copy.start()
    writes = []
    for i, (_, mid, dst) in enumerate(plan):
        reads[i].wait()
        if dst is not None:
            writes.append(pltpu.make_async_copy(mid, dst, write.at[i]))
            writes[-1].start()
        else:
            rows, width = em_out.shape
            for row in range(0, rows, 8):
                em_out[row:row + 8, :] = em_in[row // 2:row // 2 + 4].reshape(8, width)
            writes.append(pltpu.make_async_copy(em_out, oem, write.at[i]))
            writes[-1].start()
    for copy in writes:
        copy.wait()


def solution(mesh):
    owners, blocks = mesh.shape["dp"], mesh.shape["mp"]
    n = math.isqrt(owners)

    def shards(kv_up_grads, tok_grads, token_rows, step_count, master, moment_one, moment_two, average):
        cols, width, tokens = kv_up_grads.shape[1], tok_grads.shape[1], tok_grads.shape[0]
        rows = master.shape[1] // LANES
        half, ehalf = cols // 2, width // 2
        lines = lambda array: array.reshape(rows, LANES)
        dma, f32, bf16 = pltpu.SemaphoreType.DMA, jnp.float32, jnp.bfloat16
        any_space = pl.BlockSpec(memory_space=pltpu.HBM)
        state = jax.ShapeDtypeStruct((rows, LANES), f32)
        share = half // LANES + 2

        def body(*refs):
            step_kernel(n, blocks, cols, width, *refs)

        outs = pl.pallas_call(
            body,
            out_shape=(
                jax.ShapeDtypeStruct((n, n, ROWS, cols), bf16),
                jax.ShapeDtypeStruct((n, n, 2, width), bf16),
                state, state, state, state,
            ),
            in_specs=[any_space] * 3 + [pl.BlockSpec(memory_space=pltpu.SMEM)] + [any_space] * 4,
            out_specs=[any_space] * 6,
            scratch_shapes=[
                pltpu.VMEM((2, 3, n, ROWS, half), bf16),
                pltpu.VMEM((2, 2, 2, n, ROWS, half), bf16),
                pltpu.VMEM((2, 2, n // 2, ROWS, half), bf16),
                pltpu.VMEM((2, n, ROWS, half), f32),
                pltpu.VMEM((2, n, ROWS, half), f32),
                pltpu.VMEM((2, tokens, ehalf), bf16),
                pltpu.VMEM((2, 1, tokens), jnp.int32),
                pltpu.VMEM((n, 2 * n, ehalf), f32),
                pltpu.VMEM((2, 2 * n, ehalf), f32),
                pltpu.VMEM((2, 2 * n, ehalf), f32),
                pltpu.VMEM((2, n, ehalf), f32),
                pltpu.VMEM((2, 2 * n, ehalf), f32),
                pltpu.VMEM((2, 2 * n, ehalf), f32),
                pltpu.VMEM((share, n * ROWS, LANES), f32),
                pltpu.VMEM((n, share, ROWS, LANES), f32),
                pltpu.VMEM((2, share, ROWS, LANES), f32),
                pltpu.VMEM((4, rows, LANES), f32),
                pltpu.VMEM((4, rows, LANES), f32),
                pltpu.VMEM((n, 1, LANES), f32),
                pltpu.VMEM((n, 1, LANES), f32),
                pltpu.VMEM((2, blocks, 1, LANES), f32),
                pltpu.VMEM((2, 2 * (ehalf // LANES), LANES), f32),
                pltpu.VMEM((n, n, ROWS, cols), bf16),
                pltpu.VMEM((n, n, 2, width), bf16),
                dma((4,)), dma((4,)), dma((6,)),
                dma((3, 6)), dma((2, 3)), dma((2, 2, 2)), dma((2, 2)), dma((2,)), dma((2,)),
                dma((3, 2)), dma((2,)), dma((2,)), dma((2,)), dma((2,)), dma((2,)),
                dma((n,)), dma((n,)), dma((2,)),
                dma((n,)), dma((n,)), dma((n,)), dma((n,)),
                dma((2 * blocks,)), dma((2, blocks)),
                dma((2, n)), dma((2, n)),
                dma((2, 2)), dma((2,)), dma((2, n)), dma((2, 2)), dma((2,)), dma((2,)),
                dma((2, 2)), dma((2,)), dma((2,)), dma((2, 2)), dma((2,)), dma((2,)),
                dma((2, n)), dma((2, n)), dma((2, 2, n)),
            ],
            compiler_params=pltpu.CompilerParams(
                collective_id=0, has_side_effects=True
            ),
            name="adam_step",
        )(
            kv_up_grads.reshape(n, n, ROWS, cols), tok_grads, token_rows.reshape(1, tokens), step_count,
            lines(master), lines(moment_one), lines(moment_two), lines(average),
        )
        new_kv_up, new_embed, *states = outs
        new_kv_up, new_embed, *states = pl.pallas_call(
            write_out,
            out_shape=(
                jax.ShapeDtypeStruct(new_kv_up.shape, bf16), jax.ShapeDtypeStruct((owners * 2, width), bf16),
                state, state, state, state,
            ),
            in_specs=[any_space] * 6,
            out_specs=[any_space] * 6,
            scratch_shapes=[
                pltpu.VMEM((4, n // 4, n, ROWS, cols), bf16),
                pltpu.VMEM((owners, 2, width), bf16),
                pltpu.VMEM((owners * 2, width), bf16),
                pltpu.VMEM((4, rows, LANES), f32),
                dma((9,)), dma((9,)),
            ],
            name="write_out",
        )(new_kv_up, new_embed.reshape(owners, 2, width), *states)
        return (
            new_kv_up.reshape(owners * ROWS, cols),
            new_embed,
            *[array.reshape(1, rows * LANES) for array in states],
        )

    placed = (
        P(("group", "dp"), "mp"),
        P(("group", "dp"), None),
        P(("group", "dp")),
        P(),
        P("mp", "dp"),
        P("mp", "dp"),
        P("mp", "dp"),
        P("mp", "dp"),
    )
    return jax.shard_map(
        shards,
        mesh=mesh,
        in_specs=placed,
        out_specs=(
            P(None, "mp"),
            P("mp", None),
            P("mp", "dp"),
            P("mp", "dp"),
            P("mp", "dp"),
            P("mp", "dp"),
        ),
        check_vma=False,
    )
```

```python
import math

import jax
import jax.numpy as jnp
import numpy as np
from jax import lax
from jax.experimental import pallas as pl
from jax.experimental.pallas import tpu as pltpu
from jax.sharding import PartitionSpec as P

BETA_ONE = 0.9
BETA_TWO = 0.95
LEARN_RATE = 0.02
DECAY_RATE = 0.1
EPSILON = 1e-08
CLIP_NORM = 1.0
AVG_DECAY = 0.9

MESH = pl.DeviceIdType.MESH
LANES = 128
ROWS = 8


def step_kernel(
    n, nx, cols, width,
    kv, tok, trow, step, master, moment_one, moment_two, average,
    gkv, gem, omaster, omoment_one, omoment_two, oaverage,
    near, far, farh, hop, hop_in, toks, rows, part, enear, efar, efarh, ehop, ehop_in,
    share, share_in, grads, state, norm_a, norm_b, norm_c, wem,
    state_sem, tok_sem, kv_send, near_recv, far_recv, farh_recv, hop_send, hop_recv,
    em_send, enear_recv, efar_recv, efarh_recv, ehop_send, ehop_recv,
    s2_send, s2_recv, g_sem, na_send, na_recv, nb_send, nb_recv, nc_send, nc_recv,
    ga_send, ga_recv, gb_send, gb_near, gb_two, gb_fwd, gb_third, gb_four,
    ge_send, ge_near, ge_two, ge_fwd, ge_third, ge_four, gc_send, gc_recv,
):
    group = lax.axis_index("group")
    owner = lax.axis_index("dp")
    block = lax.axis_index("mp")
    y, z = owner // n, owner % n
    other = 1 - group
    half, ehalf = cols // 2, width // 2
    chunks, echunks = half // LANES, ehalf // LANES
    one = y * other + z * group
    two = z * other + y * group
    sides = ((0, 1), (1, n - 1))

    def along_y(place):
        return place * n + z

    def along_z(place):
        return y * n + place

    def along_one(place):
        return along_y(place) * other + along_z(place) * group

    def along_two(place):
        return along_z(place) * other + along_y(place) * group

    def each(body):
        def wrapped(k, _):
            body(k)
            return 0

        lax.fori_loop(1, n, wrapped, 0)

    def near_first(i):
        return (i // 2 + 1) * (1 - i % 2) + (n - 1 - i // 2) * (i % 2)

    def in_order(body):
        def wrapped(i, _):
            body(near_first(i))
            return 0

        lax.fori_loop(0, n - 1, wrapped, 0)

    def far_first(body):
        def wrapped(i, _):
            body(near_first(n - 2 - i))
            return 0

        lax.fori_loop(0, n - 1, wrapped, 0)

    def remote(src, dst, send, recv, device):
        return pltpu.make_async_remote_copy(
            src_ref=src, dst_ref=dst, send_sem=send, recv_sem=recv, device_id=device, device_id_type=MESH
        )

    partner = (other, owner, block)

    def arrive(dst, recv):
        remote(dst, dst, g_sem.at[0], recv, partner).wait_recv()

    def land(dst, sem):
        pltpu.make_async_copy(dst, dst, sem).wait()

    states = [
        pltpu.make_async_copy(ref, state.at[i], state_sem.at[i])
        for i, ref in enumerate((master, moment_one, moment_two, average))
    ]
    ecols = pl.ds(pl.multiple_of(group * ehalf, ehalf), ehalf)
    ecols_other = pl.ds(pl.multiple_of(other * ehalf, ehalf), ehalf)
    tok_here = pltpu.make_async_copy(tok.at[:, ecols], toks.at[group], tok_sem.at[4])
    row_here = pltpu.make_async_copy(trow, rows.at[group], tok_sem.at[5])
    tok_here.start()
    row_here.start()

    barrier = pltpu.get_barrier_semaphore()

    def greet(k):
        pl.semaphore_signal(barrier, inc=1, device_id=(group, along_one((one + k) % n), block), device_id_type=MESH)
        pl.semaphore_signal(barrier, inc=1, device_id=(group, along_two((two + k) % n), block), device_id_type=MESH)

    far_first(greet)
    for k in (2, n - 2, 1, n - 1):
        pl.semaphore_signal(barrier, inc=1, device_id=(other, along_one((one + k) % n), block), device_id_type=MESH)
    for k in range(1, nx):
        for core in range(2):
            pl.semaphore_signal(barrier, inc=1, device_id=(core, owner, (block + k) % nx), device_id_type=MESH)
    pl.semaphore_signal(barrier, inc=1, device_id=partner, device_id_type=MESH)
    pl.semaphore_wait(barrier, 2 * (n - 1) + 4 + 2 * (nx - 1) + 1)

    def kv_share(h, place):
        if h == 0:
            return kv.at[place, :, :, pl.ds(0, half)]
        return kv.at[:, place, :, pl.ds(half, half)]

    def kv_part(h, place, side):
        if h == 0:
            return kv.at[place, pl.ds(side * (n // 2), n // 2), :, pl.ds(0, half)]
        return kv.at[pl.ds(side * (n // 2), n // 2), place, :, pl.ds(half, half)]

    here = (y, z)
    away = (lambda place: (0, along_y(place), block), lambda place: (1, along_z(place), block))
    out = []
    for h in range(2):
        at = here[h]
        for side, sign in sides:
            out.append(remote(
                kv_part(h, (at + 4) % n, side), farh.at[side, group],
                kv_send.at[h, side], farh_recv.at[side, group], away[h]((at + 2 * sign) % n),
            ))
    for h in range(2):
        at = here[h]
        for side, sign in sides:
            out.append(remote(
                kv_share(h, (at + 3 * sign) % n), far.at[side, group, 1],
                kv_send.at[h, 2 + side], far_recv.at[side, group, 1], away[h]((at + sign) % n),
            ))
    for copy in out:
        copy.start()
    for h in range(2):
        at = here[h]
        kept = [(far.at[side, group, 0], far_recv.at[side, group, 0], (at + 2 * sign) % n) for side, sign in sides]
        kept.append((near.at[group, 0], near_recv.at[group, 0], at))

        @pl.when(group == h)
        def _(h=h, kept=kept):
            for dst, sem, place in kept:
                pltpu.make_async_copy(kv_share(h, place), dst, sem).start()

        @pl.when(group != h)
        def _(h=h, kept=kept):
            for i, (dst, sem, place) in enumerate(kept):
                remote(kv_share(h, place), dst, kv_send.at[2, i], sem, partner).start()

    tok_there = remote(tok.at[:, ecols_other], toks.at[group], tok_sem.at[0], tok_sem.at[1], partner)
    row_there = remote(trow, rows.at[group], tok_sem.at[2], tok_sem.at[3], partner)
    tok_there.start()
    row_there.start()
    for h in range(2):
        at = here[h]
        for side, sign in sides:
            copy = remote(
                kv_share(h, (at + sign) % n), near.at[group, 1 + side],
                kv_send.at[h, 4 + side], near_recv.at[group, 1 + side], away[h]((at + sign) % n),
            )
            copy.start()
            out.append(copy)
    for copy in states:
        copy.start()

    tok_here.wait()
    row_here.wait()
    tok_there.wait_recv()
    row_there.wait_recv()
    index = lax.broadcasted_iota(jnp.int32, (2 * n * n, 1), 0)
    first, second, pair = index // (2 * n), index % n, (index // n) % 2
    yy = first * other + second * group
    zz = second * other + first * group
    wanted = block * (2 * n * n) + 2 * (yy * n + zz) + pair
    total = jnp.zeros((2 * n * n, ehalf), jnp.float32)
    for core in range(2):
        onehot = jnp.where(wanted == rows[core], 1.0, 0.0).astype(jnp.bfloat16)
        total = total + jnp.dot(onehot, toks[core], preferred_element_type=jnp.float32)
    part[...] = total.reshape(n, 2 * n, ehalf)

    def ring(place):
        return (group, along_one(place % n), block)

    eout = []
    for side, sign in sides:
        eout.append(remote(
            part.at[(one + 4) % n, pl.ds(side * n, n)], efarh.at[side],
            em_send.at[0, side], efarh_recv.at[side], ring(one + 2 * sign),
        ))
    for side, sign in sides:
        eout.append(remote(
            part.at[(one + 3 * sign) % n], efar.at[side], em_send.at[1, side], efar_recv.at[side], ring(one + sign),
        ))
    for side, sign in sides:
        eout.append(remote(
            part.at[(one + sign) % n], enear.at[side], em_send.at[2, side], enear_recv.at[side], ring(one + sign),
        ))
    for copy in eout:
        copy.start()

    hops, ehops = [], []
    for side, sign in sides:
        land(far.at[side, group, 0], far_recv.at[side, group, 0])
        arrive(far.at[side, other, 0], far_recv.at[side, other, 0])
        for core in range(2):
            arrive(far.at[side, core, 1], far_recv.at[side, core, 1])
            arrive(farh.at[side, core], farh_recv.at[side, core])
        low = side * (n // 2)

        def add_four(row, _, side=side):
            for c in range(chunks):
                span = pl.ds(c * LANES, LANES)
                acc = far[side, 0, 0, row, :, span].astype(jnp.float32)
                for core, source in ((1, 0), (0, 1), (1, 1)):
                    acc = acc + far[side, core, source, row, :, span].astype(jnp.float32)
                hop[side, row, :, span] = acc
            return 0

        def add_six(i, _, side=side, low=low):
            row = low + i
            for c in range(chunks):
                span = pl.ds(c * LANES, LANES)
                acc = far[side, 0, 0, row, :, span].astype(jnp.float32)
                for core, source in ((1, 0), (0, 1), (1, 1)):
                    acc = acc + far[side, core, source, row, :, span].astype(jnp.float32)
                for core in range(2):
                    acc = acc + farh[side, core, i, :, span].astype(jnp.float32)
                hop[side, row, :, span] = acc
            return 0

        lax.fori_loop(n // 2 - low, n - low, add_four, 0)
        lax.fori_loop(0, n // 2, add_six, 0)
        copy = remote(hop.at[side], hop_in.at[side], hop_send.at[side], hop_recv.at[side], ring(one + 2 * sign))
        copy.start()
        hops.append(copy)

    for side, sign in sides:
        arrive(efar.at[side], efar_recv.at[side])
        arrive(efarh.at[side], efarh_recv.at[side])
        to = (one + 2 * sign) % n
        for i in range(2):
            at = pl.ds(i * n, n)
            if i == side:
                ehop[side, at, :] = part[to, at, :] + efar[side, at, :] + efarh[side]
            else:
                ehop[side, at, :] = part[to, at, :] + efar[side, at, :]
        copy = remote(ehop.at[side], ehop_in.at[side], ehop_send.at[side], ehop_recv.at[side], ring(one + 2 * sign))
        copy.start()
        ehops.append(copy)

    land(near.at[group, 0], near_recv.at[group, 0])
    arrive(near.at[other, 0], near_recv.at[other, 0])
    for core in range(2):
        for side in range(2):
            arrive(near.at[core, 1 + side], near_recv.at[core, 1 + side])

    def add_near(row, _):
        at = pl.ds(pl.multiple_of(row * ROWS, ROWS), ROWS)
        for c in range(chunks):
            span = pl.ds(c * LANES, LANES)
            acc = near[0, 0, row, :, span].astype(jnp.float32)
            for core, source in ((1, 0), (0, 1), (1, 1), (0, 2), (1, 2)):
                acc = acc + near[core, source, row, :, span].astype(jnp.float32)
            share[c, at, :] = acc
        return 0

    lax.fori_loop(0, n, add_near, 0)
    for side in range(2):
        arrive(enear.at[side], enear_recv.at[side])
    enear[0] = part[one] + enear[0] + enear[1]
    for side in range(2):
        arrive(hop_in.at[side], hop_recv.at[side])

    def add_hops(row, _):
        at = pl.ds(pl.multiple_of(row * ROWS, ROWS), ROWS)
        for c in range(chunks):
            span = pl.ds(c * LANES, LANES)
            share[c, at, :] = share[c, at, :] + hop_in[0, row, :, span] + hop_in[1, row, :, span]
        return 0

    lax.fori_loop(0, n, add_hops, 0)

    spans = (pl.ds(0, chunks), pl.ds(chunks, 2))

    def send_share(kind, k):
        place = (two + k) % n
        return remote(
            share.at[spans[kind], pl.ds(pl.multiple_of(place * ROWS, ROWS), ROWS), :],
            share_in.at[two, spans[kind]], s2_send.at[kind, k], s2_recv.at[kind, two], (group, along_two(place), block),
        )

    far_first(lambda k: send_share(0, k).start())
    for side in range(2):
        arrive(ehop_in.at[side], ehop_recv.at[side])
    for c in range(echunks):
        span = pl.ds(c * LANES, LANES)
        for i in range(2):
            at = pl.ds(i * n, n)
            piece = enear[0, at, span] + ehop_in[0, at, span] + ehop_in[1, at, span]
            share[chunks + i, pl.ds(c, n, stride=ROWS), :] = piece

    far_first(lambda k: send_share(1, k).start())
    share_in[two] = share[:, pl.ds(pl.multiple_of(two * ROWS, ROWS), ROWS), :]

    def wait_share(k):
        place = (two + k) % n
        for kind in range(2):
            arrive(share_in.at[place, spans[kind]], s2_recv.at[kind, place])

    in_order(wait_share)
    mine = share_in[0]
    for place in range(1, n):
        mine = mine + share_in[place]
    grads[group] = mine
    swap = remote(grads.at[group], grads.at[group], g_sem.at[0], g_sem.at[1], partner)
    swap.start()

    squares = mine * mine
    lanes = squares[0]
    for c in range(1, chunks + 2):
        lanes = lanes + squares[c]
    norm_a[y] = jnp.sum(lanes, axis=0, keepdims=True)

    def send_a(k):
        place = (y + k) % n
        return remote(norm_a.at[y], norm_a.at[y], na_send.at[k], na_recv.at[y], (group, along_y(place), block))

    def wait_a(k):
        place = (y + k) % n
        arrive(norm_a.at[place], na_recv.at[place])

    far_first(lambda k: send_a(k).start())
    in_order(wait_a)
    partial = norm_a[0]
    for place in range(1, n):
        partial = partial + norm_a[place]
    norm_b[z] = partial

    def send_b(k):
        place = (z + k) % n
        return remote(norm_b.at[z], norm_b.at[z], nb_send.at[k], nb_recv.at[z], (group, along_z(place), block))

    def wait_b(k):
        place = (z + k) % n
        arrive(norm_b.at[place], nb_recv.at[place])

    far_first(lambda k: send_b(k).start())
    in_order(wait_b)
    partial = norm_b[0]
    for place in range(1, n):
        partial = partial + norm_b[place]
    norm_c[group, block] = partial

    def send_c(k, core):
        place = (block + k) % nx
        to = group if core == 0 else other
        slot = 2 * k + core
        return remote(
            norm_c.at[group, block], norm_c.at[group, block], nc_send.at[slot], nc_recv.at[group, block], (to, owner, place)
        )

    fan = [(k, core) for k in range(nx) for core in range(2) if k or core]
    for k, core in fan:
        send_c(k, core).start()
    for k, core in fan:
        place = (block + k) % nx
        source = group if core == 0 else other
        arrive(norm_c.at[source, place], nc_recv.at[source, place])
    partial = jnp.zeros((1, LANES), jnp.float32)
    for core in range(2):
        for place in range(nx):
            partial = partial + norm_c[core, place]
    norm_value = jnp.sqrt(jnp.sum(partial, axis=1, keepdims=True))
    factor = CLIP_NORM / jnp.maximum(norm_value, CLIP_NORM)

    swap.wait_recv()
    for copy in states:
        copy.wait()

    step_float = jnp.full((1, LANES), step[0], jnp.int32).astype(jnp.float32)
    one_scale = 1.0 - jnp.exp(step_float * math.log(np.float32(BETA_ONE)))
    two_scale = 1.0 - jnp.exp(step_float * math.log(np.float32(BETA_TWO)))

    def update(at, gradient):
        clipped = factor * gradient
        weight = state[0, at, :]
        new_one = BETA_ONE * state[1, at, :] + (1.0 - BETA_ONE) * clipped
        new_two = BETA_TWO * state[2, at, :] + (1.0 - BETA_TWO) * clipped * clipped
        first_hat = new_one / one_scale
        second_hat = new_two / two_scale
        new_weight = weight - LEARN_RATE * (first_hat / (jnp.sqrt(second_hat) + EPSILON) + DECAY_RATE * weight)
        omaster[at, :] = new_weight
        omoment_one[at, :] = new_one
        omoment_two[at, :] = new_two
        oaverage[at, :] = AVG_DECAY * state[3, at, :] + (1.0 - AVG_DECAY) * new_weight
        return new_weight

    row_chunks = cols // LANES
    for h in range(2):
        for c in range(chunks):
            span = pl.ds(h * half + c * LANES, LANES)
            new = update(pl.ds(h * chunks + c, ROWS, stride=row_chunks), grads[h, c])

            @pl.when(group == h)
            def _(new=new, span=span):
                gkv[y, z, :, span] = new.astype(jnp.bfloat16)

        for i in range(2):
            at = pl.ds(ROWS * row_chunks + (i * 2 + h) * echunks, echunks)
            wem[h, pl.ds(i * echunks, echunks), :] = update(at, grads[h, chunks + i, 0:echunks, :])

    for c in range(echunks):
        for h in range(2):
            @pl.when(group == h)
            def _(h=h, c=c):
                gem[y, z, :, pl.ds(h * ehalf + c * LANES, LANES)] = wem[h, pl.ds(c, 2, stride=echunks), :].astype(jnp.bfloat16)

    kcols = pl.ds(pl.multiple_of(group * half, half), half)

    def block_of(ref, place_one, place_two, span):
        return ref.at[place_one * other + place_two * group, place_two * other + place_one * group, :, span]

    def gather_one(ref, span, kind, k):
        place = (one + k) % n
        mine = block_of(ref, one, two, span)
        return remote(mine, mine, ga_send.at[kind, k], ga_recv.at[kind, one], (group, along_one(place), block))

    def came_one(ref, span, kind, place):
        arrive(block_of(ref, place, two, span), ga_recv.at[kind, place])

    def second(place):
        return (group, along_two(place % n), block)

    def spread(place):
        ref = block_of(gkv, place, two, kcols)
        for side, sign in sides:
            remote(ref, ref, gb_send.at[1, side], gb_two.at[side, place], second(two + 2 * sign)).start()
        for side, sign in sides:
            remote(ref, ref, gb_send.at[0, side], gb_near.at[side], second(two + sign)).start()

    def half_cols(side):
        return pl.ds(pl.multiple_of(group * half + side * (half // 2), half // 2), half // 2)

    def forward(place):
        for side, sign in sides:
            source = (two - 2 * sign + 2 * n) % n
            ref = block_of(gkv, place, source, kcols)
            arrive(ref, gb_two.at[side, place])
            remote(ref, ref, gb_fwd.at[0, side], gb_third.at[side], second(two + sign)).start()
            ref = block_of(gkv, place, source, half_cols(side))
            remote(ref, ref, gb_fwd.at[1, side], gb_four.at[side], second(two + 2 * sign)).start()

    def line(ref, core, place, side=None):
        wide = ref.shape[3] // 2
        span = pl.ds(core * wide, wide) if side is None else pl.ds(core * wide + side * (wide // 2), wide // 2)
        return ref.at[:, place, :, span] if core == 0 else ref.at[place, :, :, span]

    far_first(lambda k: gather_one(gkv, kcols, 0, k).start())
    far_first(lambda k: gather_one(gem, ecols, 1, k).start())
    spread(one)

    def relay(k):
        place = (one + k) % n
        came_one(gkv, kcols, 0, place)
        spread(place)

    in_order(relay)
    in_order(lambda k: came_one(gem, ecols, 1, (one + k) % n))

    results = ((0, gkv), (1, gem))
    for core in range(2):
        @pl.when(group == core)
        def _(core=core):
            def hand_over(place):
                for kind, ref in results:
                    mine = line(ref, core, place)
                    remote(mine, mine, gc_send.at[kind, place], gc_recv.at[kind, place], partner).start()

            mine = line(gem, core, two)
            for side, sign in sides:
                remote(mine, mine, ge_send.at[1, side], ge_two.at[side], second(two + 2 * sign)).start()
            for side, sign in sides:
                remote(mine, mine, ge_send.at[0, side], ge_near.at[side], second(two + sign)).start()
            hand_over(two)
            forward(one)
            in_order(lambda k: forward((one + k) % n))
            for side, sign in sides:
                source = (two - 2 * sign + 2 * n) % n
                ref = line(gem, core, source)
                arrive(ref, ge_two.at[side])
                remote(ref, ref, ge_fwd.at[0, side], ge_third.at[side], second(two + sign)).start()
                ref = line(gem, core, source, side)
                remote(ref, ref, ge_fwd.at[1, side], ge_four.at[side], second(two + 2 * sign)).start()
            for side, sign in sides:
                source = (two - sign + n) % n
                arrive(line(gkv, core, source), gb_near.at[side])
                arrive(line(gem, core, source), ge_near.at[side])
                hand_over(source)
            for side, sign in sides:
                hand_over((two - 2 * sign + 2 * n) % n)
            for side, sign in sides:
                source = (two - 3 * sign + 3 * n) % n
                arrive(line(gkv, core, source), gb_third.at[side])
                arrive(line(gem, core, source), ge_third.at[side])
                hand_over(source)
            source = (two + 4) % n
            for side, sign in sides:
                arrive(line(gkv, core, source, side), gb_four.at[side])
                arrive(line(gem, core, source, side), ge_four.at[side])
            hand_over(source)

            def take(place, _):
                for kind, ref in results:
                    theirs = line(ref, 1 - core, place)
                    arrive(theirs, gc_recv.at[kind, place])
                return 0

            lax.fori_loop(0, n, take, 0)

            def sent_lines(place, _):
                for kind, ref in results:
                    mine = line(ref, core, place)
                    remote(mine, mine, gc_send.at[kind, place], gc_recv.at[kind, place], partner).wait_send()
                return 0

            lax.fori_loop(0, n, sent_lines, 0)
            for side in range(2):
                for i in range(2):
                    for ref, sends in ((gkv, gb_send), (gem, ge_send)):
                        mine = line(ref, core, two)
                        remote(mine, mine, sends.at[i, side], g_sem.at[1], partner).wait_send()
                for ref, sends in ((gkv, gb_fwd), (gem, ge_fwd)):
                    mine = line(ref, core, two)
                    remote(mine, mine, sends.at[0, side], g_sem.at[1], partner).wait_send()
                    mine = line(ref, core, two, side)
                    remote(mine, mine, sends.at[1, side], g_sem.at[1], partner).wait_send()

    for copy in out + eout + hops + ehops:
        copy.wait_send()
    for i in range(3):
        remote(near.at[0, 0], near.at[0, 0], kv_send.at[2, i], g_sem.at[1], partner).wait_send()
    tok_there.wait_send()
    row_there.wait_send()
    swap.wait_send()

    def sent(k):
        send_share(0, k).wait_send()
        send_share(1, k).wait_send()
        send_a(k).wait_send()
        send_b(k).wait_send()
        gather_one(gkv, kcols, 0, k).wait_send()
        gather_one(gem, ecols, 1, k).wait_send()

    each(sent)
    for k, core in fan:
        send_c(k, core).wait_send()


def write_out(kv, em, *refs):
    states, (okv, oem), out_states, em_out, sem = refs[:4], refs[4:6], refs[6:10], refs[10], refs[11]
    writes = [pltpu.make_async_copy(kv, okv, sem.at[0])]
    writes += [pltpu.make_async_copy(states[i], out_states[i], sem.at[1 + i]) for i in range(4)]
    for copy in writes:
        copy.start()
    rows, width = em_out.shape
    cut = rows // 4
    for i in range(4):
        for row in range(i * cut, (i + 1) * cut, 8):
            em_out[row:row + 8, :] = em[row // 2:row // 2 + 4].reshape(8, width)
        writes.append(pltpu.make_async_copy(em_out.at[pl.ds(i * cut, cut)], oem.at[pl.ds(i * cut, cut)], sem.at[5 + i]))
        writes[-1].start()
    for copy in writes:
        copy.wait()


def solution(mesh):
    owners, blocks = mesh.shape["dp"], mesh.shape["mp"]
    n = math.isqrt(owners)

    def shards(kv_up_grads, tok_grads, token_rows, step_count, master, moment_one, moment_two, average):
        cols, width, tokens = kv_up_grads.shape[1], tok_grads.shape[1], tok_grads.shape[0]
        rows = master.shape[1] // LANES
        half, ehalf = cols // 2, width // 2
        lines = lambda array: array.reshape(rows, LANES)
        dma, f32, bf16 = pltpu.SemaphoreType.DMA, jnp.float32, jnp.bfloat16
        any_space = pl.BlockSpec(memory_space=pltpu.HBM)
        vmem = pl.BlockSpec(memory_space=pltpu.VMEM)
        stay = lambda array: pltpu.with_memory_space_constraint(array, pltpu.HBM)
        state = jax.ShapeDtypeStruct((rows, LANES), f32)
        share = half // LANES + 2

        def body(*refs):
            step_kernel(n, blocks, cols, width, *refs)

        outs = pl.pallas_call(
            body,
            out_shape=(
                jax.ShapeDtypeStruct((n, n, ROWS, cols), bf16),
                jax.ShapeDtypeStruct((n, n, 2, width), bf16),
                state, state, state, state,
            ),
            in_specs=[any_space] * 3 + [pl.BlockSpec(memory_space=pltpu.SMEM)] + [any_space] * 4,
            out_specs=[vmem] * 6,
            scratch_shapes=[
                pltpu.VMEM((2, 3, n, ROWS, half), bf16),
                pltpu.VMEM((2, 2, 2, n, ROWS, half), bf16),
                pltpu.VMEM((2, 2, n // 2, ROWS, half), bf16),
                pltpu.VMEM((2, n, ROWS, half), f32),
                pltpu.VMEM((2, n, ROWS, half), f32),
                pltpu.VMEM((2, tokens, ehalf), bf16),
                pltpu.VMEM((2, 1, tokens), jnp.int32),
                pltpu.VMEM((n, 2 * n, ehalf), f32),
                pltpu.VMEM((2, 2 * n, ehalf), f32),
                pltpu.VMEM((2, 2 * n, ehalf), f32),
                pltpu.VMEM((2, n, ehalf), f32),
                pltpu.VMEM((2, 2 * n, ehalf), f32),
                pltpu.VMEM((2, 2 * n, ehalf), f32),
                pltpu.VMEM((share, n * ROWS, LANES), f32),
                pltpu.VMEM((n, share, ROWS, LANES), f32),
                pltpu.VMEM((2, share, ROWS, LANES), f32),
                pltpu.VMEM((4, rows, LANES), f32),
                pltpu.VMEM((n, 1, LANES), f32),
                pltpu.VMEM((n, 1, LANES), f32),
                pltpu.VMEM((2, blocks, 1, LANES), f32),
                pltpu.VMEM((2, 2 * (ehalf // LANES), LANES), f32),
                dma((4,)), dma((6,)),
                dma((3, 6)), dma((2, 3)), dma((2, 2, 2)), dma((2, 2)), dma((2,)), dma((2,)),
                dma((3, 2)), dma((2,)), dma((2,)), dma((2,)), dma((2,)), dma((2,)),
                dma((2, n)), dma((2, n)), dma((2,)),
                dma((n,)), dma((n,)), dma((n,)), dma((n,)),
                dma((2 * blocks,)), dma((2, blocks)),
                dma((2, n)), dma((2, n)),
                dma((2, 2)), dma((2,)), dma((2, n)), dma((2, 2)), dma((2,)), dma((2,)),
                dma((2, 2)), dma((2,)), dma((2,)), dma((2, 2)), dma((2,)), dma((2,)),
                dma((2, n)), dma((2, n)),
            ],
            compiler_params=pltpu.CompilerParams(
                collective_id=0, has_side_effects=True, vmem_limit_bytes=48 * 1024 * 1024
            ),
            name="adam_step",
        )(
            stay(kv_up_grads.reshape(n, n, ROWS, cols)), stay(tok_grads), stay(token_rows.reshape(1, tokens)), step_count,
            stay(lines(master)), stay(lines(moment_one)), stay(lines(moment_two)), stay(lines(average)),
        )
        new_kv_up, new_embed, *states = outs
        new_kv_up, new_embed, *states = pl.pallas_call(
            write_out,
            out_shape=(
                jax.ShapeDtypeStruct(new_kv_up.shape, bf16), jax.ShapeDtypeStruct((owners * 2, width), bf16),
                state, state, state, state,
            ),
            in_specs=[vmem] * 6,
            out_specs=[any_space] * 6,
            scratch_shapes=[pltpu.VMEM((owners * 2, width), bf16), dma((9,))],
            compiler_params=pltpu.CompilerParams(vmem_limit_bytes=16 * 1024 * 1024),
            name="write_out",
        )(new_kv_up, new_embed.reshape(owners, 2, width), *states)
        return (
            new_kv_up.reshape(owners * ROWS, cols),
            new_embed,
            *[array.reshape(1, rows * LANES) for array in states],
        )

    placed = (
        P(("group", "dp"), "mp"),
        P(("group", "dp"), None),
        P(("group", "dp")),
        P(),
        P("mp", "dp"),
        P("mp", "dp"),
        P("mp", "dp"),
        P("mp", "dp"),
    )
    return jax.shard_map(
        shards,
        mesh=mesh,
        in_specs=placed,
        out_specs=(
            P(None, "mp"),
            P("mp", None),
            P("mp", "dp"),
            P("mp", "dp"),
            P("mp", "dp"),
            P("mp", "dp"),
        ),
        check_vma=False,
    )
```

```python
import math

import jax
import jax.numpy as jnp
import numpy as np
from jax import lax
from jax.experimental import pallas as pl
from jax.experimental.pallas import tpu as pltpu
from jax.sharding import PartitionSpec as P

BETA_ONE = 0.9
BETA_TWO = 0.95
LEARN_RATE = 0.02
DECAY_RATE = 0.1
EPSILON = 1e-08
CLIP_NORM = 1.0
AVG_DECAY = 0.9

MESH = pl.DeviceIdType.MESH
LANES = 128
ROWS = 8


def step_kernel(
    n, nx, cols, width,
    kv, tok, trow, step, master, moment_one, moment_two, average,
    gkv, gem, omaster, omoment_one, omoment_two, oaverage,
    near, far, farh, hop, hop_in, toks, rows, part, enear, efar, efarh, ehop, ehop_in,
    share, share_in, grads, state, norm_a, norm_b, norm_c, wem,
    state_sem, tok_sem, kv_send, near_recv, far_recv, farh_recv, hop_send, hop_recv,
    em_send, enear_recv, efar_recv, efarh_recv, ehop_send, ehop_recv,
    s2_send, s2_recv, g_sem, na_send, na_recv, nb_send, nb_recv, nc_send, nc_recv,
    ga_send, ga_recv, gb_send, gb_near, gb_two, gb_fwd, gb_third, gb_four,
    ge_send, ge_near, ge_two, ge_fwd, ge_third, ge_four, gc_send, gc_recv, known,
):
    group = lax.axis_index("group")
    owner = lax.axis_index("dp")
    block = lax.axis_index("mp")
    y, z = owner // n, owner % n
    other = 1 - group
    half, ehalf = cols // 2, width // 2
    chunks, echunks = half // LANES, ehalf // LANES
    one = y * other + z * group
    two = z * other + y * group
    sides = ((0, 1), (1, n - 1))

    def along_y(place):
        return place * n + z

    def along_z(place):
        return y * n + place

    def along_one(place):
        return along_y(place) * other + along_z(place) * group

    def along_two(place):
        return along_z(place) * other + along_y(place) * group

    def each(body):
        def wrapped(k, _):
            body(k)
            return 0

        lax.fori_loop(1, n, wrapped, 0)

    def near_first(i):
        return (i // 2 + 1) * (1 - i % 2) + (n - 1 - i // 2) * (i % 2)

    def in_order(body):
        def wrapped(i, _):
            body(near_first(i))
            return 0

        lax.fori_loop(0, n - 1, wrapped, 0)

    def far_first(body):
        def wrapped(i, _):
            body(near_first(n - 2 - i))
            return 0

        lax.fori_loop(0, n - 1, wrapped, 0)

    def remote(src, dst, send, recv, device):
        return pltpu.make_async_remote_copy(
            src_ref=src, dst_ref=dst, send_sem=send, recv_sem=recv, device_id=device, device_id_type=MESH
        )

    partner = (other, owner, block)

    def arrive(dst, recv):
        remote(dst, dst, g_sem.at[0], recv, partner).wait_recv()

    def land(dst, sem):
        pltpu.make_async_copy(dst, dst, sem).wait()

    states = [
        pltpu.make_async_copy(ref, state.at[i], state_sem.at[i])
        for i, ref in enumerate((master, moment_one, moment_two, average))
    ]
    ecols = pl.ds(pl.multiple_of(group * ehalf, ehalf), ehalf)
    ecols_other = pl.ds(pl.multiple_of(other * ehalf, ehalf), ehalf)
    tok_here = pltpu.make_async_copy(tok.at[:, ecols], toks.at[group], tok_sem.at[4])
    row_here = pltpu.make_async_copy(trow, rows.at[group], tok_sem.at[5])
    tok_here.start()
    row_here.start()

    def kv_share(h, place):
        if h == 0:
            return kv.at[place, :, :, pl.ds(0, half)]
        return kv.at[:, place, :, pl.ds(half, half)]

    def kv_part(h, place, side):
        if h == 0:
            return kv.at[place, pl.ds(side * (n // 2), n // 2), :, pl.ds(0, half)]
        return kv.at[pl.ds(side * (n // 2), n // 2), place, :, pl.ds(half, half)]

    here = (y, z)
    kept = []
    for h in range(2):
        at = here[h]
        kept.append([(far.at[side, group, 0], far_recv.at[side, group, 0], (at + 2 * sign) % n) for side, sign in sides])
        kept[h].append((near.at[group, 0], near_recv.at[group, 0], at))

        @pl.when(group == h)
        def _(h=h):
            for dst, sem, place in kept[h]:
                pltpu.make_async_copy(kv_share(h, place), dst, sem).start()

    barrier = pltpu.get_barrier_semaphore()
    for k in (2, n - 2, 1, n - 1):
        for core in (group, other):
            pl.semaphore_signal(barrier, inc=1, device_id=(core, along_one((one + k) % n), block), device_id_type=MESH)
    for k in range(1, nx):
        for core in range(2):
            pl.semaphore_signal(barrier, inc=1, device_id=(core, owner, (block + k) % nx), device_id_type=MESH)
    pl.semaphore_signal(barrier, inc=1, device_id=partner, device_id_type=MESH)
    pl.semaphore_wait(barrier, 8 + 2 * (nx - 1) + 1)

    away = (lambda place: (0, along_y(place), block), lambda place: (1, along_z(place), block))
    out = []
    for h in range(2):
        at = here[h]
        for side, sign in sides:
            out.append(remote(
                kv_part(h, (at + 4) % n, side), farh.at[side, group],
                kv_send.at[h, side], farh_recv.at[side, group], away[h]((at + 2 * sign) % n),
            ))
    for h in range(2):
        at = here[h]
        for side, sign in sides:
            out.append(remote(
                kv_share(h, (at + 3 * sign) % n), far.at[side, group, 1],
                kv_send.at[h, 2 + side], far_recv.at[side, group, 1], away[h]((at + sign) % n),
            ))
    for copy in out:
        copy.start()
    for h in range(2):
        @pl.when(group != h)
        def _(h=h):
            for i, (dst, sem, place) in enumerate(kept[h]):
                remote(kv_share(h, place), dst, kv_send.at[2, i], sem, partner).start()

    tok_there = remote(tok.at[:, ecols_other], toks.at[group], tok_sem.at[0], tok_sem.at[1], partner)
    row_there = remote(trow, rows.at[group], tok_sem.at[2], tok_sem.at[3], partner)
    tok_there.start()
    row_there.start()
    for h in range(2):
        at = here[h]
        for side, sign in sides:
            copy = remote(
                kv_share(h, (at + sign) % n), near.at[group, 1 + side],
                kv_send.at[h, 4 + side], near_recv.at[group, 1 + side], away[h]((at + sign) % n),
            )
            copy.start()
            out.append(copy)
    for copy in states:
        copy.start()

    tok_here.wait()
    row_here.wait()
    tok_there.wait_recv()
    row_there.wait_recv()
    index = lax.broadcasted_iota(jnp.int32, (2 * n * n, 1), 0)
    first, second, pair = index // (2 * n), index % n, (index // n) % 2
    yy = first * other + second * group
    zz = second * other + first * group
    wanted = block * (2 * n * n) + 2 * (yy * n + zz) + pair
    total = jnp.zeros((2 * n * n, ehalf), jnp.float32)
    for core in range(2):
        onehot = jnp.where(wanted == rows[core], 1.0, 0.0).astype(jnp.bfloat16)
        total = total + jnp.dot(onehot, toks[core], preferred_element_type=jnp.float32)
    part[...] = total.reshape(n, 2 * n, ehalf)

    def ring(place):
        return (group, along_one(place % n), block)

    eout = []
    for side, sign in sides:
        eout.append(remote(
            part.at[(one + 4) % n, pl.ds(side * n, n)], efarh.at[side],
            em_send.at[0, side], efarh_recv.at[side], ring(one + 2 * sign),
        ))
    for side, sign in sides:
        eout.append(remote(
            part.at[(one + 3 * sign) % n], efar.at[side], em_send.at[1, side], efar_recv.at[side], ring(one + sign),
        ))
    for side, sign in sides:
        eout.append(remote(
            part.at[(one + sign) % n], enear.at[side], em_send.at[2, side], enear_recv.at[side], ring(one + sign),
        ))
    for copy in eout:
        copy.start()

    hops, ehops = [], []
    for side, sign in sides:
        land(far.at[side, group, 0], far_recv.at[side, group, 0])
        arrive(far.at[side, other, 0], far_recv.at[side, other, 0])
        for core in range(2):
            arrive(far.at[side, core, 1], far_recv.at[side, core, 1])
            arrive(farh.at[side, core], farh_recv.at[side, core])
        low = side * (n // 2)

        def add_four(row, _, side=side):
            for c in range(chunks):
                span = pl.ds(c * LANES, LANES)
                acc = far[side, 0, 0, row, :, span].astype(jnp.float32)
                for core, source in ((1, 0), (0, 1), (1, 1)):
                    acc = acc + far[side, core, source, row, :, span].astype(jnp.float32)
                hop[side, row, :, span] = acc
            return 0

        def add_six(i, _, side=side, low=low):
            row = low + i
            for c in range(chunks):
                span = pl.ds(c * LANES, LANES)
                acc = far[side, 0, 0, row, :, span].astype(jnp.float32)
                for core, source in ((1, 0), (0, 1), (1, 1)):
                    acc = acc + far[side, core, source, row, :, span].astype(jnp.float32)
                for core in range(2):
                    acc = acc + farh[side, core, i, :, span].astype(jnp.float32)
                hop[side, row, :, span] = acc
            return 0

        lax.fori_loop(n // 2 - low, n - low, add_four, 0)
        lax.fori_loop(0, n // 2, add_six, 0)
        copy = remote(hop.at[side], hop_in.at[side], hop_send.at[side], hop_recv.at[side], ring(one + 2 * sign))
        copy.start()
        hops.append(copy)

    for side, sign in sides:
        arrive(efar.at[side], efar_recv.at[side])
        arrive(efarh.at[side], efarh_recv.at[side])
        to = (one + 2 * sign) % n
        for i in range(2):
            at = pl.ds(i * n, n)
            if i == side:
                ehop[side, at, :] = part[to, at, :] + efar[side, at, :] + efarh[side]
            else:
                ehop[side, at, :] = part[to, at, :] + efar[side, at, :]
        copy = remote(ehop.at[side], ehop_in.at[side], ehop_send.at[side], ehop_recv.at[side], ring(one + 2 * sign))
        copy.start()
        ehops.append(copy)

    land(near.at[group, 0], near_recv.at[group, 0])
    arrive(near.at[other, 0], near_recv.at[other, 0])
    for core in range(2):
        for side in range(2):
            arrive(near.at[core, 1 + side], near_recv.at[core, 1 + side])

    def add_near(row, _):
        at = pl.ds(pl.multiple_of(row * ROWS, ROWS), ROWS)
        for c in range(chunks):
            span = pl.ds(c * LANES, LANES)
            acc = near[0, 0, row, :, span].astype(jnp.float32)
            for core, source in ((1, 0), (0, 1), (1, 1), (0, 2), (1, 2)):
                acc = acc + near[core, source, row, :, span].astype(jnp.float32)
            share[c, at, :] = acc
        return 0

    lax.fori_loop(0, n, add_near, 0)
    for side in range(2):
        arrive(enear.at[side], enear_recv.at[side])
    enear[0] = part[one] + enear[0] + enear[1]
    for side in range(2):
        arrive(hop_in.at[side], hop_recv.at[side])
    pl.semaphore_signal(known, inc=1, device_id=partner, device_id_type=MESH)

    def add_hops(row, _):
        at = pl.ds(pl.multiple_of(row * ROWS, ROWS), ROWS)
        for c in range(chunks):
            span = pl.ds(c * LANES, LANES)
            share[c, at, :] = share[c, at, :] + hop_in[0, row, :, span] + hop_in[1, row, :, span]
        return 0

    lax.fori_loop(0, n, add_hops, 0)

    spans = (pl.ds(0, chunks), pl.ds(chunks, 2))

    def send_share(kind, k):
        place = (two + k) % n
        return remote(
            share.at[spans[kind], pl.ds(pl.multiple_of(place * ROWS, ROWS), ROWS), :],
            share_in.at[two, spans[kind]], s2_send.at[kind, k], s2_recv.at[kind, two], (group, along_two(place), block),
        )

    pl.semaphore_wait(known, 1)
    far_first(lambda k: send_share(0, k).start())
    for side in range(2):
        arrive(ehop_in.at[side], ehop_recv.at[side])
    for c in range(echunks):
        span = pl.ds(c * LANES, LANES)
        for i in range(2):
            at = pl.ds(i * n, n)
            piece = enear[0, at, span] + ehop_in[0, at, span] + ehop_in[1, at, span]
            share[chunks + i, pl.ds(c, n, stride=ROWS), :] = piece

    far_first(lambda k: send_share(1, k).start())
    share_in[two] = share[:, pl.ds(pl.multiple_of(two * ROWS, ROWS), ROWS), :]

    def wait_share(k):
        place = (two + k) % n
        for kind in range(2):
            arrive(share_in.at[place, spans[kind]], s2_recv.at[kind, place])

    in_order(wait_share)
    mine = share_in[0]
    for place in range(1, n):
        mine = mine + share_in[place]
    grads[group] = mine
    swap = remote(grads.at[group], grads.at[group], g_sem.at[0], g_sem.at[1], partner)
    swap.start()

    squares = mine * mine
    lanes = squares[0]
    for c in range(1, chunks + 2):
        lanes = lanes + squares[c]
    norm_a[y] = jnp.sum(lanes, axis=0, keepdims=True)

    def send_a(k):
        place = (y + k) % n
        return remote(norm_a.at[y], norm_a.at[y], na_send.at[k], na_recv.at[y], (group, along_y(place), block))

    def wait_a(k):
        place = (y + k) % n
        arrive(norm_a.at[place], na_recv.at[place])

    far_first(lambda k: send_a(k).start())
    for copy in out + eout + hops + ehops:
        copy.wait_send()
    for i in range(3):
        remote(near.at[0, 0], near.at[0, 0], kv_send.at[2, i], g_sem.at[1], partner).wait_send()
    tok_there.wait_send()
    row_there.wait_send()
    in_order(wait_a)
    partial = norm_a[0]
    for place in range(1, n):
        partial = partial + norm_a[place]
    norm_b[z] = partial

    def send_b(k):
        place = (z + k) % n
        return remote(norm_b.at[z], norm_b.at[z], nb_send.at[k], nb_recv.at[z], (group, along_z(place), block))

    def wait_b(k):
        place = (z + k) % n
        arrive(norm_b.at[place], nb_recv.at[place])

    far_first(lambda k: send_b(k).start())
    for kind in range(2):
        each(lambda k: send_share(kind, k).wait_send())
    each(lambda k: send_a(k).wait_send())
    swap.wait()
    for copy in states:
        copy.wait()
    in_order(wait_b)
    partial = norm_b[0]
    for place in range(1, n):
        partial = partial + norm_b[place]
    norm_c[group, block] = partial

    def send_c(k, core):
        place = (block + k) % nx
        to = group if core == 0 else other
        slot = 2 * k + core
        return remote(
            norm_c.at[group, block], norm_c.at[group, block], nc_send.at[slot], nc_recv.at[group, block], (to, owner, place)
        )

    fan = [(k, core) for k in range(nx) for core in range(2) if k or core]
    for k, core in fan:
        send_c(k, core).start()
    each(lambda k: send_b(k).wait_send())
    step_float = jnp.full((1, LANES), step[0], jnp.int32).astype(jnp.float32)
    one_scale = 1.0 - jnp.exp(step_float * math.log(np.float32(BETA_ONE)))
    two_scale = 1.0 - jnp.exp(step_float * math.log(np.float32(BETA_TWO)))
    for k, core in fan:
        place = (block + k) % nx
        source = group if core == 0 else other
        arrive(norm_c.at[source, place], nc_recv.at[source, place])
    partial = jnp.zeros((1, LANES), jnp.float32)
    for core in range(2):
        for place in range(nx):
            partial = partial + norm_c[core, place]
    norm_value = jnp.sqrt(jnp.sum(partial, axis=1, keepdims=True))
    factor = CLIP_NORM / jnp.maximum(norm_value, CLIP_NORM)

    def update(at, gradient):
        clipped = factor * gradient
        weight = state[0, at, :]
        new_one = BETA_ONE * state[1, at, :] + (1.0 - BETA_ONE) * clipped
        new_two = BETA_TWO * state[2, at, :] + (1.0 - BETA_TWO) * clipped * clipped
        first_hat = new_one / one_scale
        second_hat = new_two / two_scale
        new_weight = weight - LEARN_RATE * (first_hat / (jnp.sqrt(second_hat) + EPSILON) + DECAY_RATE * weight)
        omaster[at, :] = new_weight
        omoment_one[at, :] = new_one
        omoment_two[at, :] = new_two
        oaverage[at, :] = AVG_DECAY * state[3, at, :] + (1.0 - AVG_DECAY) * new_weight
        return new_weight

    row_chunks = cols // LANES
    for h in range(2):
        for c in range(chunks):
            span = pl.ds(h * half + c * LANES, LANES)
            new = update(pl.ds(h * chunks + c, ROWS, stride=row_chunks), grads[h, c])

            @pl.when(group == h)
            def _(new=new, span=span):
                gkv[y, z, :, span] = new.astype(jnp.bfloat16)

        for i in range(2):
            at = pl.ds(ROWS * row_chunks + (i * 2 + h) * echunks, echunks)
            wem[h, pl.ds(i * echunks, echunks), :] = update(at, grads[h, chunks + i, 0:echunks, :])

    for c in range(echunks):
        for h in range(2):
            @pl.when(group == h)
            def _(h=h, c=c):
                gem[y, z, :, pl.ds(h * ehalf + c * LANES, LANES)] = wem[h, pl.ds(c, 2, stride=echunks), :].astype(jnp.bfloat16)

    kcols = pl.ds(pl.multiple_of(group * half, half), half)

    def block_of(ref, place_one, place_two, span):
        return ref.at[place_one * other + place_two * group, place_two * other + place_one * group, :, span]

    def gather_one(ref, span, kind, k):
        place = (one + k) % n
        mine = block_of(ref, one, two, span)
        return remote(mine, mine, ga_send.at[kind, k], ga_recv.at[kind, one], (group, along_one(place), block))

    def came_one(ref, span, kind, place):
        arrive(block_of(ref, place, two, span), ga_recv.at[kind, place])

    def second(place):
        return (group, along_two(place % n), block)

    def spread(place):
        ref = block_of(gkv, place, two, kcols)
        for side, sign in sides:
            remote(ref, ref, gb_send.at[1, side], gb_two.at[side, place], second(two + 2 * sign)).start()
        for side, sign in sides:
            remote(ref, ref, gb_send.at[0, side], gb_near.at[side], second(two + sign)).start()

    def half_cols(side):
        return pl.ds(pl.multiple_of(group * half + side * (half // 2), half // 2), half // 2)

    def forward(place):
        for side, sign in sides:
            source = (two - 2 * sign + 2 * n) % n
            ref = block_of(gkv, place, source, kcols)
            arrive(ref, gb_two.at[side, place])
            remote(ref, ref, gb_fwd.at[0, side], gb_third.at[side], second(two + sign)).start()
            ref = block_of(gkv, place, source, half_cols(side))
            remote(ref, ref, gb_fwd.at[1, side], gb_four.at[side], second(two + 2 * sign)).start()

    def line(ref, core, place, side=None):
        wide = ref.shape[3] // 2
        span = pl.ds(core * wide, wide) if side is None else pl.ds(core * wide + side * (wide // 2), wide // 2)
        return ref.at[:, place, :, span] if core == 0 else ref.at[place, :, :, span]

    far_first(lambda k: gather_one(gkv, kcols, 0, k).start())
    far_first(lambda k: gather_one(gem, ecols, 1, k).start())
    spread(one)

    def relay(k):
        place = (one + k) % n
        came_one(gkv, kcols, 0, place)
        spread(place)

    in_order(relay)
    in_order(lambda k: came_one(gem, ecols, 1, (one + k) % n))

    results = ((0, gkv), (1, gem))
    for core in range(2):
        @pl.when(group == core)
        def _(core=core):
            def hand_over(place, kinds=results):
                for kind, ref in kinds:
                    mine = line(ref, core, place)
                    remote(mine, mine, gc_send.at[kind, place], gc_recv.at[kind, place], partner).start()

            mine = line(gem, core, two)
            for side, sign in sides:
                remote(mine, mine, ge_send.at[1, side], ge_two.at[side], second(two + 2 * sign)).start()
            for side, sign in sides:
                remote(mine, mine, ge_send.at[0, side], ge_near.at[side], second(two + sign)).start()
            each(lambda k: gather_one(gkv, kcols, 0, k).wait_send())
            each(lambda k: gather_one(gem, ecols, 1, k).wait_send())
            for k, to in fan:
                send_c(k, to).wait_send()
            forward(one)
            in_order(lambda k: forward((one + k) % n))
            for side, sign in sides:
                source = (two - 2 * sign + 2 * n) % n
                ref = line(gem, core, source)
                arrive(ref, ge_two.at[side])
                remote(ref, ref, ge_fwd.at[0, side], ge_third.at[side], second(two + sign)).start()
                ref = line(gem, core, source, side)
                remote(ref, ref, ge_fwd.at[1, side], ge_four.at[side], second(two + 2 * sign)).start()
            hand_over(two)
            for side, sign in sides:
                source = (two - sign + n) % n
                arrive(line(gkv, core, source), gb_near.at[side])
                arrive(line(gem, core, source), ge_near.at[side])
                hand_over(source)
            for side, sign in sides:
                hand_over((two - 2 * sign + 2 * n) % n)
            last = (two + 4) % n
            for kind in range(2):
                ref = results[kind][1]
                third, four = ((gb_third, gb_four), (ge_third, ge_four))[kind]
                for side, sign in sides:
                    source = (two - 3 * sign + 3 * n) % n
                    arrive(line(ref, core, source), third.at[side])
                    hand_over(source, results[kind:kind + 1])
                for side in range(2):
                    arrive(line(ref, core, last, side), four.at[side])
                hand_over(last, results[kind:kind + 1])

            def take(place, _):
                for kind, ref in results:
                    theirs = line(ref, 1 - core, place)
                    arrive(theirs, gc_recv.at[kind, place])
                return 0

            lax.fori_loop(0, n, take, 0)

            def sent_lines(place, _):
                for kind, ref in results:
                    mine = line(ref, core, place)
                    remote(mine, mine, gc_send.at[kind, place], gc_recv.at[kind, place], partner).wait_send()
                return 0

            lax.fori_loop(0, n, sent_lines, 0)
            for side in range(2):
                for i in range(2):
                    for ref, sends in ((gkv, gb_send), (gem, ge_send)):
                        mine = line(ref, core, two)
                        remote(mine, mine, sends.at[i, side], g_sem.at[1], partner).wait_send()
                for ref, sends in ((gkv, gb_fwd), (gem, ge_fwd)):
                    mine = line(ref, core, two)
                    remote(mine, mine, sends.at[0, side], g_sem.at[1], partner).wait_send()
                    mine = line(ref, core, two, side)
                    remote(mine, mine, sends.at[1, side], g_sem.at[1], partner).wait_send()


def write_out(kv, em, *refs):
    states, (okv, oem), out_states, em_out, sem = refs[:4], refs[4:6], refs[6:10], refs[10], refs[11]
    writes = [pltpu.make_async_copy(kv, okv, sem.at[0])]
    writes += [pltpu.make_async_copy(states[i], out_states[i], sem.at[1 + i]) for i in range(4)]
    for copy in writes:
        copy.start()
    rows, width = em_out.shape
    cut = rows // 4
    for i in range(4):
        for row in range(i * cut, (i + 1) * cut, 8):
            em_out[row:row + 8, :] = em[row // 2:row // 2 + 4].reshape(8, width)
        writes.append(pltpu.make_async_copy(em_out.at[pl.ds(i * cut, cut)], oem.at[pl.ds(i * cut, cut)], sem.at[5 + i]))
        writes[-1].start()
    for copy in writes:
        copy.wait()


def solution(mesh):
    owners, blocks = mesh.shape["dp"], mesh.shape["mp"]
    n = math.isqrt(owners)

    def shards(kv_up_grads, tok_grads, token_rows, step_count, master, moment_one, moment_two, average):
        cols, width, tokens = kv_up_grads.shape[1], tok_grads.shape[1], tok_grads.shape[0]
        rows = master.shape[1] // LANES
        half, ehalf = cols // 2, width // 2
        lines = lambda array: array.reshape(rows, LANES)
        dma, f32, bf16 = pltpu.SemaphoreType.DMA, jnp.float32, jnp.bfloat16
        any_space = pl.BlockSpec(memory_space=pltpu.HBM)
        vmem = pl.BlockSpec(memory_space=pltpu.VMEM)
        stay = lambda array: pltpu.with_memory_space_constraint(array, pltpu.HBM)
        state = jax.ShapeDtypeStruct((rows, LANES), f32)
        share = half // LANES + 2

        def body(*refs):
            step_kernel(n, blocks, cols, width, *refs)

        outs = pl.pallas_call(
            body,
            out_shape=(
                jax.ShapeDtypeStruct((n, n, ROWS, cols), bf16),
                jax.ShapeDtypeStruct((n, n, 2, width), bf16),
                state, state, state, state,
            ),
            in_specs=[any_space] * 3 + [pl.BlockSpec(memory_space=pltpu.SMEM)] + [any_space] * 4,
            out_specs=[vmem] * 6,
            scratch_shapes=[
                pltpu.VMEM((2, 3, n, ROWS, half), bf16),
                pltpu.VMEM((2, 2, 2, n, ROWS, half), bf16),
                pltpu.VMEM((2, 2, n // 2, ROWS, half), bf16),
                pltpu.VMEM((2, n, ROWS, half), f32),
                pltpu.VMEM((2, n, ROWS, half), f32),
                pltpu.VMEM((2, tokens, ehalf), bf16),
                pltpu.VMEM((2, 1, tokens), jnp.int32),
                pltpu.VMEM((n, 2 * n, ehalf), f32),
                pltpu.VMEM((2, 2 * n, ehalf), f32),
                pltpu.VMEM((2, 2 * n, ehalf), f32),
                pltpu.VMEM((2, n, ehalf), f32),
                pltpu.VMEM((2, 2 * n, ehalf), f32),
                pltpu.VMEM((2, 2 * n, ehalf), f32),
                pltpu.VMEM((share, n * ROWS, LANES), f32),
                pltpu.VMEM((n, share, ROWS, LANES), f32),
                pltpu.VMEM((2, share, ROWS, LANES), f32),
                pltpu.VMEM((4, rows, LANES), f32),
                pltpu.VMEM((n, 1, LANES), f32),
                pltpu.VMEM((n, 1, LANES), f32),
                pltpu.VMEM((2, blocks, 1, LANES), f32),
                pltpu.VMEM((2, 2 * (ehalf // LANES), LANES), f32),
                dma((4,)), dma((6,)),
                dma((3, 6)), dma((2, 3)), dma((2, 2, 2)), dma((2, 2)), dma((2,)), dma((2,)),
                dma((3, 2)), dma((2,)), dma((2,)), dma((2,)), dma((2,)), dma((2,)),
                dma((2, n)), dma((2, n)), dma((2,)),
                dma((n,)), dma((n,)), dma((n,)), dma((n,)),
                dma((2 * blocks,)), dma((2, blocks)),
                dma((2, n)), dma((2, n)),
                dma((2, 2)), dma((2,)), dma((2, n)), dma((2, 2)), dma((2,)), dma((2,)),
                dma((2, 2)), dma((2,)), dma((2,)), dma((2, 2)), dma((2,)), dma((2,)),
                dma((2, n)), dma((2, n)), pltpu.SemaphoreType.REGULAR,
            ],
            compiler_params=pltpu.CompilerParams(
                collective_id=0, has_side_effects=True, vmem_limit_bytes=48 * 1024 * 1024
            ),
            name="adam_step",
        )(
            stay(kv_up_grads.reshape(n, n, ROWS, cols)), stay(tok_grads), stay(token_rows.reshape(1, tokens)), step_count,
            stay(lines(master)), stay(lines(moment_one)), stay(lines(moment_two)), stay(lines(average)),
        )
        new_kv_up, new_embed, *states = outs
        new_kv_up, new_embed, *states = pl.pallas_call(
            write_out,
            out_shape=(
                jax.ShapeDtypeStruct(new_kv_up.shape, bf16), jax.ShapeDtypeStruct((owners * 2, width), bf16),
                state, state, state, state,
            ),
            in_specs=[vmem] * 6,
            out_specs=[any_space] * 6,
            scratch_shapes=[pltpu.VMEM((owners * 2, width), bf16), dma((9,))],
            compiler_params=pltpu.CompilerParams(vmem_limit_bytes=16 * 1024 * 1024),
            name="write_out",
        )(new_kv_up, new_embed.reshape(owners, 2, width), *states)
        return (
            new_kv_up.reshape(owners * ROWS, cols),
            new_embed,
            *[array.reshape(1, rows * LANES) for array in states],
        )

    placed = (
        P(("group", "dp"), "mp"),
        P(("group", "dp"), None),
        P(("group", "dp")),
        P(),
        P("mp", "dp"),
        P("mp", "dp"),
        P("mp", "dp"),
        P("mp", "dp"),
    )
    return jax.shard_map(
        shards,
        mesh=mesh,
        in_specs=placed,
        out_specs=(
            P(None, "mp"),
            P("mp", None),
            P("mp", "dp"),
            P("mp", "dp"),
            P("mp", "dp"),
            P("mp", "dp"),
        ),
        check_vma=False,
    )
```

```python
import math

import jax
import jax.numpy as jnp
import numpy as np
from jax import lax
from jax.experimental import pallas as pl
from jax.experimental.pallas import tpu as pltpu
from jax.sharding import PartitionSpec as P

BETA_ONE = 0.9
BETA_TWO = 0.95
LEARN_RATE = 0.02
DECAY_RATE = 0.1
EPSILON = 1e-08
CLIP_NORM = 1.0
AVG_DECAY = 0.9

MESH = pl.DeviceIdType.MESH
LANES = 128
ROWS = 8


def step_kernel(
    n, nx, cols, width,
    kv, tok, trow, step, master, moment_one, moment_two, average,
    gkv, gem, omaster, omoment_one, omoment_two, oaverage,
    near, far, farh, hop, hop_in, toks, rows, part, enear, efar, efarh, ehop, ehop_in,
    share, share_in, grads, state, lstate, lgrads, norm_a, norm_b, norm_c, wem,
    state_sem, tok_sem, kv_send, near_recv, far_recv, farh_recv, hop_send, hop_recv,
    em_send, enear_recv, efar_recv, efarh_recv, ehop_send, ehop_recv,
    s2_send, s2_recv, g_sem, na_send, na_recv, nb_send, nb_recv, nc_send, nc_recv,
    ls_send, ls_recv, lg_send, lg_recv, gb_send, gb_near, gb_two, gb_fwd, gb_third, gb_four,
    ge_send, ge_near, ge_two, ge_fwd, ge_third, ge_four, gc_send, gc_recv, known,
):
    group = lax.axis_index("group")
    owner = lax.axis_index("dp")
    block = lax.axis_index("mp")
    y, z = owner // n, owner % n
    other = 1 - group
    half, ehalf = cols // 2, width // 2
    chunks, echunks = half // LANES, ehalf // LANES
    one = y * other + z * group
    two = z * other + y * group
    sides = ((0, 1), (1, n - 1))

    def along_y(place):
        return place * n + z

    def along_z(place):
        return y * n + place

    def along_one(place):
        return along_y(place) * other + along_z(place) * group

    def along_two(place):
        return along_z(place) * other + along_y(place) * group

    def each(body):
        def wrapped(k, _):
            body(k)
            return 0

        lax.fori_loop(1, n, wrapped, 0)

    def near_first(i):
        return (i // 2 + 1) * (1 - i % 2) + (n - 1 - i // 2) * (i % 2)

    def in_order(body):
        def wrapped(i, _):
            body(near_first(i))
            return 0

        lax.fori_loop(0, n - 1, wrapped, 0)

    def far_first(body):
        def wrapped(i, _):
            body(near_first(n - 2 - i))
            return 0

        lax.fori_loop(0, n - 1, wrapped, 0)

    def remote(src, dst, send, recv, device):
        return pltpu.make_async_remote_copy(
            src_ref=src, dst_ref=dst, send_sem=send, recv_sem=recv, device_id=device, device_id_type=MESH
        )

    partner = (other, owner, block)

    def arrive(dst, recv):
        remote(dst, dst, g_sem.at[0], recv, partner).wait_recv()

    def land(dst, sem):
        pltpu.make_async_copy(dst, dst, sem).wait()

    states = [
        pltpu.make_async_copy(ref, state.at[i], state_sem.at[i])
        for i, ref in enumerate((master, moment_one, moment_two, average))
    ]
    ecols = pl.ds(pl.multiple_of(group * ehalf, ehalf), ehalf)
    ecols_other = pl.ds(pl.multiple_of(other * ehalf, ehalf), ehalf)
    tok_here = pltpu.make_async_copy(tok.at[:, ecols], toks.at[group], tok_sem.at[4])
    row_here = pltpu.make_async_copy(trow, rows.at[group], tok_sem.at[5])
    tok_here.start()
    row_here.start()

    def kv_share(h, place):
        if h == 0:
            return kv.at[place, :, :, pl.ds(0, half)]
        return kv.at[:, place, :, pl.ds(half, half)]

    def kv_part(h, place, side):
        if h == 0:
            return kv.at[place, pl.ds(side * (n // 2), n // 2), :, pl.ds(0, half)]
        return kv.at[pl.ds(side * (n // 2), n // 2), place, :, pl.ds(half, half)]

    here = (y, z)
    kept = []
    for h in range(2):
        at = here[h]
        kept.append([(far.at[side, group, 0], far_recv.at[side, group, 0], (at + 2 * sign) % n) for side, sign in sides])
        kept[h].append((near.at[group, 0], near_recv.at[group, 0], at))

        @pl.when(group == h)
        def _(h=h):
            for dst, sem, place in kept[h]:
                pltpu.make_async_copy(kv_share(h, place), dst, sem).start()

    barrier = pltpu.get_barrier_semaphore()
    for k in (2, n - 2, 1, n - 1):
        for core in (group, other):
            pl.semaphore_signal(barrier, inc=1, device_id=(core, along_one((one + k) % n), block), device_id_type=MESH)
    for k in range(1, nx):
        for core in range(2):
            pl.semaphore_signal(barrier, inc=1, device_id=(core, owner, (block + k) % nx), device_id_type=MESH)
    pl.semaphore_signal(barrier, inc=1, device_id=partner, device_id_type=MESH)
    pl.semaphore_wait(barrier, 8 + 2 * (nx - 1) + 1)

    away = (lambda place: (0, along_y(place), block), lambda place: (1, along_z(place), block))
    out = []
    for h in range(2):
        at = here[h]
        for side, sign in sides:
            out.append(remote(
                kv_part(h, (at + 4) % n, side), farh.at[side, group],
                kv_send.at[h, side], farh_recv.at[side, group], away[h]((at + 2 * sign) % n),
            ))
    for h in range(2):
        at = here[h]
        for side, sign in sides:
            out.append(remote(
                kv_share(h, (at + 3 * sign) % n), far.at[side, group, 1],
                kv_send.at[h, 2 + side], far_recv.at[side, group, 1], away[h]((at + sign) % n),
            ))
    for copy in out:
        copy.start()
    for h in range(2):
        @pl.when(group != h)
        def _(h=h):
            for i, (dst, sem, place) in enumerate(kept[h]):
                remote(kv_share(h, place), dst, kv_send.at[2, i], sem, partner).start()

    tok_there = remote(tok.at[:, ecols_other], toks.at[group], tok_sem.at[0], tok_sem.at[1], partner)
    row_there = remote(trow, rows.at[group], tok_sem.at[2], tok_sem.at[3], partner)
    tok_there.start()
    row_there.start()
    for h in range(2):
        at = here[h]
        for side, sign in sides:
            copy = remote(
                kv_share(h, (at + sign) % n), near.at[group, 1 + side],
                kv_send.at[h, 4 + side], near_recv.at[group, 1 + side], away[h]((at + sign) % n),
            )
            copy.start()
            out.append(copy)
    for copy in states:
        copy.start()

    tok_here.wait()
    row_here.wait()
    tok_there.wait_recv()
    row_there.wait_recv()
    index = lax.broadcasted_iota(jnp.int32, (2 * n * n, 1), 0)
    first, second, pair = index // (2 * n), index % n, (index // n) % 2
    yy = first * other + second * group
    zz = second * other + first * group
    wanted = block * (2 * n * n) + 2 * (yy * n + zz) + pair
    total = jnp.zeros((2 * n * n, ehalf), jnp.float32)
    for core in range(2):
        onehot = jnp.where(wanted == rows[core], 1.0, 0.0).astype(jnp.bfloat16)
        total = total + jnp.dot(onehot, toks[core], preferred_element_type=jnp.float32)
    part[...] = total.reshape(n, 2 * n, ehalf)

    def ring(place):
        return (group, along_one(place % n), block)

    eout = []
    for side, sign in sides:
        eout.append(remote(
            part.at[(one + 4) % n, pl.ds(side * n, n)], efarh.at[side],
            em_send.at[0, side], efarh_recv.at[side], ring(one + 2 * sign),
        ))
    for side, sign in sides:
        eout.append(remote(
            part.at[(one + 3 * sign) % n], efar.at[side], em_send.at[1, side], efar_recv.at[side], ring(one + sign),
        ))
    for side, sign in sides:
        eout.append(remote(
            part.at[(one + sign) % n], enear.at[side], em_send.at[2, side], enear_recv.at[side], ring(one + sign),
        ))
    for copy in eout:
        copy.start()

    hops, ehops = [], []
    for side, sign in sides:
        land(far.at[side, group, 0], far_recv.at[side, group, 0])
        arrive(far.at[side, other, 0], far_recv.at[side, other, 0])
        for core in range(2):
            arrive(far.at[side, core, 1], far_recv.at[side, core, 1])
            arrive(farh.at[side, core], farh_recv.at[side, core])
        low = side * (n // 2)

        def add_four(row, _, side=side):
            for c in range(chunks):
                span = pl.ds(c * LANES, LANES)
                acc = far[side, 0, 0, row, :, span].astype(jnp.float32)
                for core, source in ((1, 0), (0, 1), (1, 1)):
                    acc = acc + far[side, core, source, row, :, span].astype(jnp.float32)
                hop[side, row, :, span] = acc
            return 0

        def add_six(i, _, side=side, low=low):
            row = low + i
            for c in range(chunks):
                span = pl.ds(c * LANES, LANES)
                acc = far[side, 0, 0, row, :, span].astype(jnp.float32)
                for core, source in ((1, 0), (0, 1), (1, 1)):
                    acc = acc + far[side, core, source, row, :, span].astype(jnp.float32)
                for core in range(2):
                    acc = acc + farh[side, core, i, :, span].astype(jnp.float32)
                hop[side, row, :, span] = acc
            return 0

        lax.fori_loop(n // 2 - low, n - low, add_four, 0)
        lax.fori_loop(0, n // 2, add_six, 0)
        copy = remote(hop.at[side], hop_in.at[side], hop_send.at[side], hop_recv.at[side], ring(one + 2 * sign))
        copy.start()
        hops.append(copy)

    for side, sign in sides:
        arrive(efar.at[side], efar_recv.at[side])
        arrive(efarh.at[side], efarh_recv.at[side])
        to = (one + 2 * sign) % n
        for i in range(2):
            at = pl.ds(i * n, n)
            if i == side:
                ehop[side, at, :] = part[to, at, :] + efar[side, at, :] + efarh[side]
            else:
                ehop[side, at, :] = part[to, at, :] + efar[side, at, :]
        copy = remote(ehop.at[side], ehop_in.at[side], ehop_send.at[side], ehop_recv.at[side], ring(one + 2 * sign))
        copy.start()
        ehops.append(copy)

    land(near.at[group, 0], near_recv.at[group, 0])
    arrive(near.at[other, 0], near_recv.at[other, 0])
    for core in range(2):
        for side in range(2):
            arrive(near.at[core, 1 + side], near_recv.at[core, 1 + side])

    def add_near(row, _):
        at = pl.ds(pl.multiple_of(row * ROWS, ROWS), ROWS)
        for c in range(chunks):
            span = pl.ds(c * LANES, LANES)
            acc = near[0, 0, row, :, span].astype(jnp.float32)
            for core, source in ((1, 0), (0, 1), (1, 1), (0, 2), (1, 2)):
                acc = acc + near[core, source, row, :, span].astype(jnp.float32)
            share[c, at, :] = acc
        return 0

    lax.fori_loop(0, n, add_near, 0)
    for side in range(2):
        arrive(enear.at[side], enear_recv.at[side])
    enear[0] = part[one] + enear[0] + enear[1]
    for side in range(2):
        arrive(hop_in.at[side], hop_recv.at[side])
    pl.semaphore_signal(known, inc=1, device_id=partner, device_id_type=MESH)

    def add_hops(row, _):
        at = pl.ds(pl.multiple_of(row * ROWS, ROWS), ROWS)
        for c in range(chunks):
            span = pl.ds(c * LANES, LANES)
            share[c, at, :] = share[c, at, :] + hop_in[0, row, :, span] + hop_in[1, row, :, span]
        return 0

    lax.fori_loop(0, n, add_hops, 0)

    spans = (pl.ds(0, chunks), pl.ds(chunks, 2))

    def send_share(kind, k):
        place = (two + k) % n
        return remote(
            share.at[spans[kind], pl.ds(pl.multiple_of(place * ROWS, ROWS), ROWS), :],
            share_in.at[two, spans[kind]], s2_send.at[kind, k], s2_recv.at[kind, two], (group, along_two(place), block),
        )

    pl.semaphore_wait(known, 1)
    far_first(lambda k: send_share(0, k).start())

    row_chunks = cols // LANES
    for copy in states:
        copy.wait()

    def place_of(h, t):
        if t < chunks:
            return pl.ds(h * chunks + t, ROWS, stride=row_chunks)
        return pl.ds(ROWS * row_chunks + ((t - chunks) * 2 + h) * echunks, echunks)

    for h in range(2):
        @pl.when(group == h)
        def _(h=h):
            for a in range(3):
                for t in range(chunks + 2):
                    lstate[one, a, t] = state[a, place_of(h, t), :]

    def send_state(a, k):
        return remote(lstate.at[one, a], lstate.at[one, a], ls_send.at[a, k], ls_recv.at[a, one], ring(one + k))

    def send_grads(k):
        return remote(lgrads.at[one], lgrads.at[one], lg_send.at[k], lg_recv.at[one], ring(one + k))

    for side in range(2):
        arrive(ehop_in.at[side], ehop_recv.at[side])
    for c in range(echunks):
        span = pl.ds(c * LANES, LANES)
        for i in range(2):
            at = pl.ds(i * n, n)
            piece = enear[0, at, span] + ehop_in[0, at, span] + ehop_in[1, at, span]
            share[chunks + i, pl.ds(c, n, stride=ROWS), :] = piece

    far_first(lambda k: send_share(1, k).start())
    far_first(lambda k: send_state(0, k).start())
    share_in[two] = share[:, pl.ds(pl.multiple_of(two * ROWS, ROWS), ROWS), :]

    def wait_share(k):
        place = (two + k) % n
        for kind in range(2):
            arrive(share_in.at[place, spans[kind]], s2_recv.at[kind, place])

    in_order(wait_share)
    mine = share_in[0]
    for place in range(1, n):
        mine = mine + share_in[place]
    grads[group] = mine
    lgrads[one] = mine
    swap = remote(grads.at[group], grads.at[group], g_sem.at[0], g_sem.at[1], partner)
    swap.start()

    squares = mine * mine
    lanes = squares[0]
    for c in range(1, chunks + 2):
        lanes = lanes + squares[c]
    norm_a[y] = jnp.sum(lanes, axis=0, keepdims=True)

    def send_a(k):
        place = (y + k) % n
        return remote(norm_a.at[y], norm_a.at[y], na_send.at[k], na_recv.at[y], (group, along_y(place), block))

    def wait_a(k):
        place = (y + k) % n
        arrive(norm_a.at[place], na_recv.at[place])

    far_first(lambda k: send_a(k).start())
    far_first(lambda k: send_grads(k).start())
    far_first(lambda k: send_state(1, k).start())
    for copy in out + eout + hops + ehops:
        copy.wait_send()
    for i in range(3):
        remote(near.at[0, 0], near.at[0, 0], kv_send.at[2, i], g_sem.at[1], partner).wait_send()
    tok_there.wait_send()
    row_there.wait_send()
    in_order(wait_a)
    partial = norm_a[0]
    for place in range(1, n):
        partial = partial + norm_a[place]
    norm_b[z] = partial

    def send_b(k):
        place = (z + k) % n
        return remote(norm_b.at[z], norm_b.at[z], nb_send.at[k], nb_recv.at[z], (group, along_z(place), block))

    def wait_b(k):
        place = (z + k) % n
        arrive(norm_b.at[place], nb_recv.at[place])

    far_first(lambda k: send_b(k).start())
    far_first(lambda k: send_state(2, k).start())
    for kind in range(2):
        each(lambda k: send_share(kind, k).wait_send())
    each(lambda k: send_a(k).wait_send())
    swap.wait()
    in_order(wait_b)
    partial = norm_b[0]
    for place in range(1, n):
        partial = partial + norm_b[place]
    norm_c[group, block] = partial

    def send_c(k, core):
        place = (block + k) % nx
        to = group if core == 0 else other
        slot = 2 * k + core
        return remote(
            norm_c.at[group, block], norm_c.at[group, block], nc_send.at[slot], nc_recv.at[group, block], (to, owner, place)
        )

    fan = [(k, core) for k in range(nx) for core in range(2) if k or core]
    for k, core in fan:
        send_c(k, core).start()
    each(lambda k: send_b(k).wait_send())
    step_float = jnp.full((1, LANES), step[0], jnp.int32).astype(jnp.float32)
    one_scale = 1.0 - jnp.exp(step_float * math.log(np.float32(BETA_ONE)))
    two_scale = 1.0 - jnp.exp(step_float * math.log(np.float32(BETA_TWO)))
    for k, core in fan:
        place = (block + k) % nx
        source = group if core == 0 else other
        arrive(norm_c.at[source, place], nc_recv.at[source, place])
    partial = jnp.zeros((1, LANES), jnp.float32)
    for core in range(2):
        for place in range(nx):
            partial = partial + norm_c[core, place]
    norm_value = jnp.sqrt(jnp.sum(partial, axis=1, keepdims=True))
    factor = CLIP_NORM / jnp.maximum(norm_value, CLIP_NORM)

    def moments(gradient, old_one, old_two):
        clipped = factor * gradient
        new_one = BETA_ONE * old_one + (1.0 - BETA_ONE) * clipped
        new_two = BETA_TWO * old_two + (1.0 - BETA_TWO) * clipped * clipped
        return new_one, new_two

    def weight_after(weight, new_one, new_two):
        first_hat = new_one / one_scale
        second_hat = new_two / two_scale
        return weight - LEARN_RATE * (first_hat / (jnp.sqrt(second_hat) + EPSILON) + DECAY_RATE * weight)

    def come(k):
        place = (one + k) % n
        for a in range(3):
            arrive(lstate.at[place, a], ls_recv.at[a, place])
        arrive(lgrads.at[place], lg_recv.at[place])

    each(come)

    kcols = pl.ds(pl.multiple_of(group * half, half), half)

    def block_of(ref, place_one, place_two, span):
        return ref.at[place_one * other + place_two * group, place_two * other + place_one * group, :, span]

    def second(place):
        return (group, along_two(place % n), block)

    def spread(place):
        ref = block_of(gkv, place, two, kcols)
        for side, sign in sides:
            remote(ref, ref, gb_send.at[1, side], gb_two.at[side, place], second(two + 2 * sign)).start()
        for side, sign in sides:
            remote(ref, ref, gb_send.at[0, side], gb_near.at[side], second(two + sign)).start()

    def half_cols(side):
        return pl.ds(pl.multiple_of(group * half + side * (half // 2), half // 2), half // 2)

    def forward(place):
        for side, sign in sides:
            source = (two - 2 * sign + 2 * n) % n
            ref = block_of(gkv, place, source, kcols)
            arrive(ref, gb_two.at[side, place])
            remote(ref, ref, gb_fwd.at[0, side], gb_third.at[side], second(two + sign)).start()
            ref = block_of(gkv, place, source, half_cols(side))
            remote(ref, ref, gb_fwd.at[1, side], gb_four.at[side], second(two + 2 * sign)).start()

    def line(ref, core, place, side=None):
        wide = ref.shape[3] // 2
        span = pl.ds(core * wide, wide) if side is None else pl.ds(core * wide + side * (wide // 2), wide // 2)
        return ref.at[:, place, :, span] if core == 0 else ref.at[place, :, :, span]

    def make(place):
        new = []
        for t in range(chunks + 2):
            new_one, new_two = moments(lgrads[place, t], lstate[place, 1, t], lstate[place, 2, t])
            new.append(weight_after(lstate[place, 0, t], new_one, new_two))
        for i in range(2):
            wem[pl.ds(i * echunks, echunks), :] = new[chunks + i][0:echunks]
        at = (place * other + two * group, two * other + place * group)
        for h in range(2):
            @pl.when(group == h)
            def _(h=h):
                for t in range(chunks):
                    gkv[at[0], at[1], :, pl.ds(h * half + t * LANES, LANES)] = new[t].astype(jnp.bfloat16)
                for c in range(echunks):
                    span = pl.ds(h * ehalf + c * LANES, LANES)
                    gem[at[0], at[1], :, span] = wem[pl.ds(c, 2, stride=echunks), :].astype(jnp.bfloat16)

        spread(place)

    def make_all(place, _):
        make(place)
        return 0

    lax.fori_loop(0, n, make_all, 0)

    def keep_own():
        for h in range(2):
            for t in range(chunks + 2):
                at = place_of(h, t)
                weight = state[0, at, :]
                new_one, new_two = moments(grads[h, t], state[1, at, :], state[2, at, :])
                new_weight = weight_after(weight, new_one, new_two)
                omaster[at, :] = new_weight
                omoment_one[at, :] = new_one
                omoment_two[at, :] = new_two
                oaverage[at, :] = AVG_DECAY * state[3, at, :] + (1.0 - AVG_DECAY) * new_weight
        for a in range(3):
            each(lambda k: send_state(a, k).wait_send())
        each(lambda k: send_grads(k).wait_send())
        for k, to in fan:
            send_c(k, to).wait_send()

    results = ((0, gkv), (1, gem))
    for core in range(2):
        @pl.when(group == core)
        def _(core=core):
            def hand_over(place, kinds=results):
                for kind, ref in kinds:
                    mine = line(ref, core, place)
                    remote(mine, mine, gc_send.at[kind, place], gc_recv.at[kind, place], partner).start()

            mine = line(gem, core, two)
            for side, sign in sides:
                remote(mine, mine, ge_send.at[1, side], ge_two.at[side], second(two + 2 * sign)).start()
            for side, sign in sides:
                remote(mine, mine, ge_send.at[0, side], ge_near.at[side], second(two + sign)).start()
            keep_own()

            def forward_all(place, _):
                forward(place)
                return 0

            lax.fori_loop(0, n, forward_all, 0)
            for side, sign in sides:
                source = (two - 2 * sign + 2 * n) % n
                ref = line(gem, core, source)
                arrive(ref, ge_two.at[side])
                remote(ref, ref, ge_fwd.at[0, side], ge_third.at[side], second(two + sign)).start()
                ref = line(gem, core, source, side)
                remote(ref, ref, ge_fwd.at[1, side], ge_four.at[side], second(two + 2 * sign)).start()
            hand_over(two)
            for side, sign in sides:
                source = (two - sign + n) % n
                arrive(line(gkv, core, source), gb_near.at[side])
                arrive(line(gem, core, source), ge_near.at[side])
                hand_over(source)
            for side, sign in sides:
                hand_over((two - 2 * sign + 2 * n) % n)
            last = (two + 4) % n
            for kind in range(2):
                ref = results[kind][1]
                third, four = ((gb_third, gb_four), (ge_third, ge_four))[kind]
                for side, sign in sides:
                    source = (two - 3 * sign + 3 * n) % n
                    arrive(line(ref, core, source), third.at[side])
                    hand_over(source, results[kind:kind + 1])
                for side in range(2):
                    arrive(line(ref, core, last, side), four.at[side])
                hand_over(last, results[kind:kind + 1])

            def take(place, _):
                for kind, ref in results:
                    theirs = line(ref, 1 - core, place)
                    arrive(theirs, gc_recv.at[kind, place])
                return 0

            lax.fori_loop(0, n, take, 0)

            def sent_lines(place, _):
                for kind, ref in results:
                    mine = line(ref, core, place)
                    remote(mine, mine, gc_send.at[kind, place], gc_recv.at[kind, place], partner).wait_send()
                return 0

            lax.fori_loop(0, n, sent_lines, 0)
            for side in range(2):
                for i in range(2):
                    for ref, sends in ((gkv, gb_send), (gem, ge_send)):
                        mine = line(ref, core, two)
                        remote(mine, mine, sends.at[i, side], g_sem.at[1], partner).wait_send()
                for ref, sends in ((gkv, gb_fwd), (gem, ge_fwd)):
                    mine = line(ref, core, two)
                    remote(mine, mine, sends.at[0, side], g_sem.at[1], partner).wait_send()
                    mine = line(ref, core, two, side)
                    remote(mine, mine, sends.at[1, side], g_sem.at[1], partner).wait_send()


def write_out(kv, em, *refs):
    states, (okv, oem), out_states, em_out, sem = refs[:4], refs[4:6], refs[6:10], refs[10], refs[11]
    writes = [pltpu.make_async_copy(kv, okv, sem.at[0])]
    writes += [pltpu.make_async_copy(states[i], out_states[i], sem.at[1 + i]) for i in range(4)]
    for copy in writes:
        copy.start()
    rows, width = em_out.shape
    cut = rows // 4
    for i in range(4):
        for row in range(i * cut, (i + 1) * cut, 8):
            em_out[row:row + 8, :] = em[row // 2:row // 2 + 4].reshape(8, width)
        writes.append(pltpu.make_async_copy(em_out.at[pl.ds(i * cut, cut)], oem.at[pl.ds(i * cut, cut)], sem.at[5 + i]))
        writes[-1].start()
    for copy in writes:
        copy.wait()


def solution(mesh):
    owners, blocks = mesh.shape["dp"], mesh.shape["mp"]
    n = math.isqrt(owners)

    def shards(kv_up_grads, tok_grads, token_rows, step_count, master, moment_one, moment_two, average):
        cols, width, tokens = kv_up_grads.shape[1], tok_grads.shape[1], tok_grads.shape[0]
        rows = master.shape[1] // LANES
        half, ehalf = cols // 2, width // 2
        lines = lambda array: array.reshape(rows, LANES)
        dma, f32, bf16 = pltpu.SemaphoreType.DMA, jnp.float32, jnp.bfloat16
        any_space = pl.BlockSpec(memory_space=pltpu.HBM)
        vmem = pl.BlockSpec(memory_space=pltpu.VMEM)
        stay = lambda array: pltpu.with_memory_space_constraint(array, pltpu.HBM)
        state = jax.ShapeDtypeStruct((rows, LANES), f32)
        share = half // LANES + 2

        def body(*refs):
            step_kernel(n, blocks, cols, width, *refs)

        outs = pl.pallas_call(
            body,
            out_shape=(
                jax.ShapeDtypeStruct((n, n, ROWS, cols), bf16),
                jax.ShapeDtypeStruct((n, n, 2, width), bf16),
                state, state, state, state,
            ),
            in_specs=[any_space] * 3 + [pl.BlockSpec(memory_space=pltpu.SMEM)] + [any_space] * 4,
            out_specs=[vmem] * 6,
            scratch_shapes=[
                pltpu.VMEM((2, 3, n, ROWS, half), bf16),
                pltpu.VMEM((2, 2, 2, n, ROWS, half), bf16),
                pltpu.VMEM((2, 2, n // 2, ROWS, half), bf16),
                pltpu.VMEM((2, n, ROWS, half), f32),
                pltpu.VMEM((2, n, ROWS, half), f32),
                pltpu.VMEM((2, tokens, ehalf), bf16),
                pltpu.VMEM((2, 1, tokens), jnp.int32),
                pltpu.VMEM((n, 2 * n, ehalf), f32),
                pltpu.VMEM((2, 2 * n, ehalf), f32),
                pltpu.VMEM((2, 2 * n, ehalf), f32),
                pltpu.VMEM((2, n, ehalf), f32),
                pltpu.VMEM((2, 2 * n, ehalf), f32),
                pltpu.VMEM((2, 2 * n, ehalf), f32),
                pltpu.VMEM((share, n * ROWS, LANES), f32),
                pltpu.VMEM((n, share, ROWS, LANES), f32),
                pltpu.VMEM((2, share, ROWS, LANES), f32),
                pltpu.VMEM((4, rows, LANES), f32),
                pltpu.VMEM((n, 3, share, ROWS, LANES), f32),
                pltpu.VMEM((n, share, ROWS, LANES), f32),
                pltpu.VMEM((n, 1, LANES), f32),
                pltpu.VMEM((n, 1, LANES), f32),
                pltpu.VMEM((2, blocks, 1, LANES), f32),
                pltpu.VMEM((2 * (ehalf // LANES), LANES), f32),
                dma((4,)), dma((6,)),
                dma((3, 6)), dma((2, 3)), dma((2, 2, 2)), dma((2, 2)), dma((2,)), dma((2,)),
                dma((3, 2)), dma((2,)), dma((2,)), dma((2,)), dma((2,)), dma((2,)),
                dma((2, n)), dma((2, n)), dma((2,)),
                dma((n,)), dma((n,)), dma((n,)), dma((n,)),
                dma((2 * blocks,)), dma((2, blocks)),
                dma((3, n)), dma((3, n)), dma((n,)), dma((n,)),
                dma((2, 2)), dma((2,)), dma((2, n)), dma((2, 2)), dma((2,)), dma((2,)),
                dma((2, 2)), dma((2,)), dma((2,)), dma((2, 2)), dma((2,)), dma((2,)),
                dma((2, n)), dma((2, n)), pltpu.SemaphoreType.REGULAR,
            ],
            compiler_params=pltpu.CompilerParams(
                collective_id=0, has_side_effects=True, vmem_limit_bytes=48 * 1024 * 1024
            ),
            name="adam_step",
        )(
            stay(kv_up_grads.reshape(n, n, ROWS, cols)), stay(tok_grads), stay(token_rows.reshape(1, tokens)), step_count,
            stay(lines(master)), stay(lines(moment_one)), stay(lines(moment_two)), stay(lines(average)),
        )
        new_kv_up, new_embed, *states = outs
        new_kv_up, new_embed, *states = pl.pallas_call(
            write_out,
            out_shape=(
                jax.ShapeDtypeStruct(new_kv_up.shape, bf16), jax.ShapeDtypeStruct((owners * 2, width), bf16),
                state, state, state, state,
            ),
            in_specs=[vmem] * 6,
            out_specs=[any_space] * 6,
            scratch_shapes=[pltpu.VMEM((owners * 2, width), bf16), dma((9,))],
            compiler_params=pltpu.CompilerParams(vmem_limit_bytes=16 * 1024 * 1024),
            name="write_out",
        )(new_kv_up, new_embed.reshape(owners, 2, width), *states)
        return (
            new_kv_up.reshape(owners * ROWS, cols),
            new_embed,
            *[array.reshape(1, rows * LANES) for array in states],
        )

    placed = (
        P(("group", "dp"), "mp"),
        P(("group", "dp"), None),
        P(("group", "dp")),
        P(),
        P("mp", "dp"),
        P("mp", "dp"),
        P("mp", "dp"),
        P("mp", "dp"),
    )
    return jax.shard_map(
        shards,
        mesh=mesh,
        in_specs=placed,
        out_specs=(
            P(None, "mp"),
            P("mp", None),
            P("mp", "dp"),
            P("mp", "dp"),
            P("mp", "dp"),
            P("mp", "dp"),
        ),
        check_vma=False,
    )
```

```python
import math

import jax
import jax.numpy as jnp
import numpy as np
from jax import lax
from jax.experimental import pallas as pl
from jax.experimental.pallas import tpu as pltpu
from jax.sharding import PartitionSpec as P

BETA_ONE = 0.9
BETA_TWO = 0.95
LEARN_RATE = 0.02
DECAY_RATE = 0.1
EPSILON = 1e-08
CLIP_NORM = 1.0
AVG_DECAY = 0.9

MESH = pl.DeviceIdType.MESH
LANES = 128
ROWS = 8


def step_kernel(
    n, nx, cols, width,
    kv, tok, trow, step, master, moment_one, moment_two, average,
    gkv, gem, omaster, omoment_one, omoment_two, oaverage,
    near, far, farh, hop, hop_in, toks, rows, part, enear, efar, efarh, ehop, ehop_in,
    share, share_in, grads, state, lstate, lgrads, norm_a, norm_b, norm_c, wem,
    state_sem, tok_sem, kv_send, near_recv, far_recv, farh_recv, hop_send, hop_recv,
    em_send, enear_recv, efar_recv, efarh_recv, ehop_send, ehop_recv,
    s2_send, s2_recv, g_sem, na_send, na_recv, nb_send, nb_recv, nc_send, nc_recv,
    ls_send, ls_recv, lg_send, lg_recv, gb_send, gb_near, gb_two, gb_fwd, gb_third, gb_four,
    ge_send, ge_near, ge_two, ge_fwd, ge_third, ge_four, gc_send, gc_recv, known,
):
    group = lax.axis_index("group")
    owner = lax.axis_index("dp")
    block = lax.axis_index("mp")
    y, z = owner // n, owner % n
    other = 1 - group
    half, ehalf = cols // 2, width // 2
    chunks, echunks = half // LANES, ehalf // LANES
    one = y * other + z * group
    two = z * other + y * group
    sides = ((0, 1), (1, n - 1))

    def along_y(place):
        return place * n + z

    def along_z(place):
        return y * n + place

    def along_one(place):
        return along_y(place) * other + along_z(place) * group

    def along_two(place):
        return along_z(place) * other + along_y(place) * group

    def each(body):
        def wrapped(k, _):
            body(k)
            return 0

        lax.fori_loop(1, n, wrapped, 0)

    def near_first(i):
        return (i // 2 + 1) * (1 - i % 2) + (n - 1 - i // 2) * (i % 2)

    def in_order(body):
        def wrapped(i, _):
            body(near_first(i))
            return 0

        lax.fori_loop(0, n - 1, wrapped, 0)

    def far_first(body):
        def wrapped(i, _):
            body(near_first(n - 2 - i))
            return 0

        lax.fori_loop(0, n - 1, wrapped, 0)

    def remote(src, dst, send, recv, device):
        return pltpu.make_async_remote_copy(
            src_ref=src, dst_ref=dst, send_sem=send, recv_sem=recv, device_id=device, device_id_type=MESH
        )

    partner = (other, owner, block)

    def arrive(dst, recv):
        remote(dst, dst, g_sem.at[0], recv, partner).wait_recv()

    def land(dst, sem):
        pltpu.make_async_copy(dst, dst, sem).wait()

    states = [
        pltpu.make_async_copy(ref, state.at[i], state_sem.at[i])
        for i, ref in enumerate((master, moment_one, moment_two, average))
    ]
    ecols = pl.ds(pl.multiple_of(group * ehalf, ehalf), ehalf)
    ecols_other = pl.ds(pl.multiple_of(other * ehalf, ehalf), ehalf)
    tok_here = pltpu.make_async_copy(tok.at[:, ecols], toks.at[group], tok_sem.at[4])
    row_here = pltpu.make_async_copy(trow, rows.at[group], tok_sem.at[5])
    tok_here.start()
    row_here.start()

    def kv_share(h, place):
        if h == 0:
            return kv.at[place, :, :, pl.ds(0, half)]
        return kv.at[:, place, :, pl.ds(half, half)]

    def kv_part(h, place, side):
        if h == 0:
            return kv.at[place, pl.ds(side * (n // 2), n // 2), :, pl.ds(0, half)]
        return kv.at[pl.ds(side * (n // 2), n // 2), place, :, pl.ds(half, half)]

    here = (y, z)
    kept = []
    for h in range(2):
        at = here[h]
        kept.append([(far.at[side, group, 0], far_recv.at[side, group, 0], (at + 2 * sign) % n) for side, sign in sides])
        kept[h].append((near.at[group, 0], near_recv.at[group, 0], at))

        @pl.when(group == h)
        def _(h=h):
            for dst, sem, place in kept[h]:
                pltpu.make_async_copy(kv_share(h, place), dst, sem).start()

    barrier = pltpu.get_barrier_semaphore()
    for k in (2, n - 2, 1, n - 1):
        for core in (group, other):
            pl.semaphore_signal(barrier, inc=1, device_id=(core, along_one((one + k) % n), block), device_id_type=MESH)
    for k in range(1, nx):
        for core in range(2):
            pl.semaphore_signal(barrier, inc=1, device_id=(core, owner, (block + k) % nx), device_id_type=MESH)
    pl.semaphore_signal(barrier, inc=1, device_id=partner, device_id_type=MESH)
    pl.semaphore_wait(barrier, 8 + 2 * (nx - 1) + 1)

    away = (lambda place: (0, along_y(place), block), lambda place: (1, along_z(place), block))
    out = []
    for h in range(2):
        at = here[h]
        for side, sign in sides:
            out.append(remote(
                kv_part(h, (at + 4) % n, side), farh.at[side, group],
                kv_send.at[h, side], farh_recv.at[side, group], away[h]((at + 2 * sign) % n),
            ))
    for h in range(2):
        at = here[h]
        for side, sign in sides:
            out.append(remote(
                kv_share(h, (at + 3 * sign) % n), far.at[side, group, 1],
                kv_send.at[h, 2 + side], far_recv.at[side, group, 1], away[h]((at + sign) % n),
            ))
    for copy in out:
        copy.start()
    for h in range(2):
        @pl.when(group != h)
        def _(h=h):
            for i, (dst, sem, place) in enumerate(kept[h]):
                remote(kv_share(h, place), dst, kv_send.at[2, i], sem, partner).start()

    tok_there = remote(tok.at[:, ecols_other], toks.at[group], tok_sem.at[0], tok_sem.at[1], partner)
    row_there = remote(trow, rows.at[group], tok_sem.at[2], tok_sem.at[3], partner)
    tok_there.start()
    row_there.start()
    for h in range(2):
        at = here[h]
        for side, sign in sides:
            copy = remote(
                kv_share(h, (at + sign) % n), near.at[group, 1 + side],
                kv_send.at[h, 4 + side], near_recv.at[group, 1 + side], away[h]((at + sign) % n),
            )
            copy.start()
            out.append(copy)
    for copy in states:
        copy.start()

    tok_here.wait()
    row_here.wait()
    tok_there.wait_recv()
    row_there.wait_recv()
    index = lax.broadcasted_iota(jnp.int32, (2 * n * n, 1), 0)
    first, second, pair = index // (2 * n), index % n, (index // n) % 2
    yy = first * other + second * group
    zz = second * other + first * group
    wanted = block * (2 * n * n) + 2 * (yy * n + zz) + pair
    total = jnp.zeros((2 * n * n, ehalf), jnp.float32)
    for core in range(2):
        onehot = jnp.where(wanted == rows[core], 1.0, 0.0).astype(jnp.bfloat16)
        total = total + jnp.dot(onehot, toks[core], preferred_element_type=jnp.float32)
    part[...] = total.reshape(n, 2 * n, ehalf)

    def ring(place):
        return (group, along_one(place % n), block)

    eout = []
    for side, sign in sides:
        eout.append(remote(
            part.at[(one + 4) % n, pl.ds(side * n, n)], efarh.at[side],
            em_send.at[0, side], efarh_recv.at[side], ring(one + 2 * sign),
        ))
    for side, sign in sides:
        eout.append(remote(
            part.at[(one + 3 * sign) % n], efar.at[side], em_send.at[1, side], efar_recv.at[side], ring(one + sign),
        ))
    for side, sign in sides:
        eout.append(remote(
            part.at[(one + sign) % n], enear.at[side], em_send.at[2, side], enear_recv.at[side], ring(one + sign),
        ))
    for copy in eout:
        copy.start()

    hops, ehops = [], []
    for side, sign in sides:
        land(far.at[side, group, 0], far_recv.at[side, group, 0])
        arrive(far.at[side, other, 0], far_recv.at[side, other, 0])
        for core in range(2):
            arrive(far.at[side, core, 1], far_recv.at[side, core, 1])
            arrive(farh.at[side, core], farh_recv.at[side, core])
        low = side * (n // 2)

        def add_four(row, _, side=side):
            for c in range(chunks):
                span = pl.ds(c * LANES, LANES)
                acc = far[side, 0, 0, row, :, span].astype(jnp.float32)
                for core, source in ((1, 0), (0, 1), (1, 1)):
                    acc = acc + far[side, core, source, row, :, span].astype(jnp.float32)
                hop[side, row, :, span] = acc
            return 0

        def add_six(i, _, side=side, low=low):
            row = low + i
            for c in range(chunks):
                span = pl.ds(c * LANES, LANES)
                acc = far[side, 0, 0, row, :, span].astype(jnp.float32)
                for core, source in ((1, 0), (0, 1), (1, 1)):
                    acc = acc + far[side, core, source, row, :, span].astype(jnp.float32)
                for core in range(2):
                    acc = acc + farh[side, core, i, :, span].astype(jnp.float32)
                hop[side, row, :, span] = acc
            return 0

        lax.fori_loop(n // 2 - low, n - low, add_four, 0)
        lax.fori_loop(0, n // 2, add_six, 0)
        copy = remote(hop.at[side], hop_in.at[side], hop_send.at[side], hop_recv.at[side], ring(one + 2 * sign))
        copy.start()
        hops.append(copy)

    for side, sign in sides:
        arrive(efar.at[side], efar_recv.at[side])
        arrive(efarh.at[side], efarh_recv.at[side])
        to = (one + 2 * sign) % n
        for i in range(2):
            at = pl.ds(i * n, n)
            if i == side:
                ehop[side, at, :] = part[to, at, :] + efar[side, at, :] + efarh[side]
            else:
                ehop[side, at, :] = part[to, at, :] + efar[side, at, :]
        copy = remote(ehop.at[side], ehop_in.at[side], ehop_send.at[side], ehop_recv.at[side], ring(one + 2 * sign))
        copy.start()
        ehops.append(copy)

    land(near.at[group, 0], near_recv.at[group, 0])
    arrive(near.at[other, 0], near_recv.at[other, 0])
    for core in range(2):
        for side in range(2):
            arrive(near.at[core, 1 + side], near_recv.at[core, 1 + side])

    def add_near(row, _):
        at = pl.ds(pl.multiple_of(row * ROWS, ROWS), ROWS)
        for c in range(chunks):
            span = pl.ds(c * LANES, LANES)
            acc = near[0, 0, row, :, span].astype(jnp.float32)
            for core, source in ((1, 0), (0, 1), (1, 1), (0, 2), (1, 2)):
                acc = acc + near[core, source, row, :, span].astype(jnp.float32)
            share[c, at, :] = acc
        return 0

    lax.fori_loop(0, n, add_near, 0)
    for side in range(2):
        arrive(enear.at[side], enear_recv.at[side])
    enear[0] = part[one] + enear[0] + enear[1]
    for side in range(2):
        arrive(hop_in.at[side], hop_recv.at[side])
    pl.semaphore_signal(known, inc=1, device_id=partner, device_id_type=MESH)

    def add_hops(row, _):
        at = pl.ds(pl.multiple_of(row * ROWS, ROWS), ROWS)
        for c in range(chunks):
            span = pl.ds(c * LANES, LANES)
            share[c, at, :] = share[c, at, :] + hop_in[0, row, :, span] + hop_in[1, row, :, span]
        return 0

    lax.fori_loop(0, n, add_hops, 0)

    spans = (pl.ds(0, chunks), pl.ds(chunks, 2))

    def send_share(kind, k):
        place = (two + k) % n
        return remote(
            share.at[spans[kind], pl.ds(pl.multiple_of(place * ROWS, ROWS), ROWS), :],
            share_in.at[two, spans[kind]], s2_send.at[kind, k], s2_recv.at[kind, two], (group, along_two(place), block),
        )

    pl.semaphore_wait(known, 1)
    far_first(lambda k: send_share(0, k).start())

    row_chunks = cols // LANES
    for copy in states:
        copy.wait()

    def place_of(h, t):
        if t < chunks:
            return pl.ds(h * chunks + t, ROWS, stride=row_chunks)
        return pl.ds(ROWS * row_chunks + ((t - chunks) * 2 + h) * echunks, echunks)

    for h in range(2):
        @pl.when(group == h)
        def _(h=h):
            for a in range(3):
                for t in range(chunks + 2):
                    lstate[one, a, t] = state[a, place_of(h, t), :]

    def send_state(a, k):
        return remote(lstate.at[one, a], lstate.at[one, a], ls_send.at[a, k], ls_recv.at[a, one], ring(one + k))

    def send_grads(k):
        return remote(lgrads.at[one], lgrads.at[one], lg_send.at[k], lg_recv.at[one], ring(one + k))

    for side in range(2):
        arrive(ehop_in.at[side], ehop_recv.at[side])
    for c in range(echunks):
        span = pl.ds(c * LANES, LANES)
        for i in range(2):
            at = pl.ds(i * n, n)
            piece = enear[0, at, span] + ehop_in[0, at, span] + ehop_in[1, at, span]
            share[chunks + i, pl.ds(c, n, stride=ROWS), :] = piece

    far_first(lambda k: send_share(1, k).start())
    far_first(lambda k: send_state(0, k).start())
    share_in[two] = share[:, pl.ds(pl.multiple_of(two * ROWS, ROWS), ROWS), :]

    def wait_share(k):
        place = (two + k) % n
        for kind in range(2):
            arrive(share_in.at[place, spans[kind]], s2_recv.at[kind, place])

    in_order(wait_share)
    mine = share_in[0]
    for place in range(1, n):
        mine = mine + share_in[place]
    grads[group] = mine
    lgrads[one] = mine
    swap = remote(grads.at[group], grads.at[group], g_sem.at[0], g_sem.at[1], partner)
    swap.start()

    squares = mine * mine
    lanes = squares[0]
    for c in range(1, chunks + 2):
        lanes = lanes + squares[c]
    norm_a[y] = jnp.sum(lanes, axis=0, keepdims=True)

    def send_a(k):
        place = (y + k) % n
        return remote(norm_a.at[y], norm_a.at[y], na_send.at[k], na_recv.at[y], (group, along_y(place), block))

    def wait_a(k):
        place = (y + k) % n
        arrive(norm_a.at[place], na_recv.at[place])

    far_first(lambda k: send_a(k).start())
    far_first(lambda k: send_grads(k).start())
    far_first(lambda k: send_state(1, k).start())
    for copy in out + eout + hops + ehops:
        copy.wait_send()
    for i in range(3):
        remote(near.at[0, 0], near.at[0, 0], kv_send.at[2, i], g_sem.at[1], partner).wait_send()
    tok_there.wait_send()
    row_there.wait_send()
    in_order(wait_a)
    partial = norm_a[0]
    for place in range(1, n):
        partial = partial + norm_a[place]
    norm_b[z] = partial

    def send_b(k):
        place = (z + k) % n
        return remote(norm_b.at[z], norm_b.at[z], nb_send.at[k], nb_recv.at[z], (group, along_z(place), block))

    def wait_b(k):
        place = (z + k) % n
        arrive(norm_b.at[place], nb_recv.at[place])

    far_first(lambda k: send_b(k).start())
    far_first(lambda k: send_state(2, k).start())
    for kind in range(2):
        each(lambda k: send_share(kind, k).wait_send())
    each(lambda k: send_a(k).wait_send())
    swap.wait()
    in_order(wait_b)
    partial = norm_b[0]
    for place in range(1, n):
        partial = partial + norm_b[place]
    norm_c[group, block] = partial

    def send_c(k, core):
        place = (block + k) % nx
        to = group if core == 0 else other
        slot = 2 * k + core
        return remote(
            norm_c.at[group, block], norm_c.at[group, block], nc_send.at[slot], nc_recv.at[group, block], (to, owner, place)
        )

    fan = [(k, core) for k in range(nx) for core in range(2) if k or core]
    for k, core in fan:
        send_c(k, core).start()
    each(lambda k: send_b(k).wait_send())
    step_float = jnp.full((1, LANES), step[0], jnp.int32).astype(jnp.float32)
    one_scale = 1.0 - jnp.exp(step_float * math.log(np.float32(BETA_ONE)))
    two_scale = 1.0 - jnp.exp(step_float * math.log(np.float32(BETA_TWO)))
    for k, core in fan:
        place = (block + k) % nx
        source = group if core == 0 else other
        arrive(norm_c.at[source, place], nc_recv.at[source, place])
    partial = jnp.zeros((1, LANES), jnp.float32)
    for core in range(2):
        for place in range(nx):
            partial = partial + norm_c[core, place]
    norm_value = jnp.sqrt(jnp.sum(partial, axis=1, keepdims=True))
    factor = CLIP_NORM / jnp.maximum(norm_value, CLIP_NORM)

    def moments(gradient, old_one, old_two):
        clipped = factor * gradient
        new_one = BETA_ONE * old_one + (1.0 - BETA_ONE) * clipped
        new_two = BETA_TWO * old_two + (1.0 - BETA_TWO) * clipped * clipped
        return new_one, new_two

    def weight_after(weight, new_one, new_two):
        first_hat = new_one / one_scale
        second_hat = new_two / two_scale
        return weight - LEARN_RATE * (first_hat / (jnp.sqrt(second_hat) + EPSILON) + DECAY_RATE * weight)

    def come(k):
        place = (one + k) % n
        for a in range(3):
            arrive(lstate.at[place, a], ls_recv.at[a, place])
        arrive(lgrads.at[place], lg_recv.at[place])

    each(come)

    kcols = pl.ds(pl.multiple_of(group * half, half), half)

    def block_of(ref, place_one, place_two, span):
        return ref.at[place_one * other + place_two * group, place_two * other + place_one * group, :, span]

    def second(place):
        return (group, along_two(place % n), block)

    def spread(place):
        ref = block_of(gkv, place, two, kcols)
        for side, sign in sides:
            remote(ref, ref, gb_send.at[1, side], gb_two.at[side, place], second(two + 2 * sign)).start()

    def half_cols(side):
        return pl.ds(pl.multiple_of(group * half + side * (half // 2), half // 2), half // 2)

    def forward(place):
        for side, sign in sides:
            source = (two - 2 * sign + 2 * n) % n
            ref = block_of(gkv, place, source, kcols)
            arrive(ref, gb_two.at[side, place])
            remote(ref, ref, gb_fwd.at[0, side], gb_third.at[side], second(two + sign)).start()
            ref = block_of(gkv, place, source, half_cols(side))
            remote(ref, ref, gb_fwd.at[1, side], gb_four.at[side], second(two + 2 * sign)).start()

    def line(ref, core, place, side=None):
        wide = ref.shape[3] // 2
        span = pl.ds(core * wide, wide) if side is None else pl.ds(core * wide + side * (wide // 2), wide // 2)
        return ref.at[:, place, :, span] if core == 0 else ref.at[place, :, :, span]

    def make(place):
        new = []
        for t in range(chunks + 2):
            new_one, new_two = moments(lgrads[place, t], lstate[place, 1, t], lstate[place, 2, t])
            new.append(weight_after(lstate[place, 0, t], new_one, new_two))
        for i in range(2):
            wem[pl.ds(i * echunks, echunks), :] = new[chunks + i][0:echunks]
        at = (place * other + two * group, two * other + place * group)
        for h in range(2):
            @pl.when(group == h)
            def _(h=h):
                for t in range(chunks):
                    gkv[at[0], at[1], :, pl.ds(h * half + t * LANES, LANES)] = new[t].astype(jnp.bfloat16)
                for c in range(echunks):
                    span = pl.ds(h * ehalf + c * LANES, LANES)
                    gem[at[0], at[1], :, span] = wem[pl.ds(c, 2, stride=echunks), :].astype(jnp.bfloat16)

        spread(place)

    def make_all(place, _):
        make(place)
        return 0

    lax.fori_loop(0, n, make_all, 0)

    def keep_own():
        for h in range(2):
            for t in range(chunks + 2):
                at = place_of(h, t)
                weight = state[0, at, :]
                new_one, new_two = moments(grads[h, t], state[1, at, :], state[2, at, :])
                new_weight = weight_after(weight, new_one, new_two)
                omaster[at, :] = new_weight
                omoment_one[at, :] = new_one
                omoment_two[at, :] = new_two
                oaverage[at, :] = AVG_DECAY * state[3, at, :] + (1.0 - AVG_DECAY) * new_weight
        for a in range(3):
            each(lambda k: send_state(a, k).wait_send())
        each(lambda k: send_grads(k).wait_send())
        for k, to in fan:
            send_c(k, to).wait_send()

    results = ((0, gkv), (1, gem))
    for core in range(2):
        @pl.when(group == core)
        def _(core=core):
            def hand_over(place, kinds=results):
                for kind, ref in kinds:
                    mine = line(ref, core, place)
                    remote(mine, mine, gc_send.at[kind, place], gc_recv.at[kind, place], partner).start()

            mine = line(gem, core, two)
            for side, sign in sides:
                remote(mine, mine, ge_send.at[1, side], ge_two.at[side], second(two + 2 * sign)).start()
            for side, sign in sides:
                for ref, sends, comes in ((gkv, gb_send, gb_near), (gem, ge_send, ge_near)):
                    mine = line(ref, core, two)
                    remote(mine, mine, sends.at[0, side], comes.at[side], second(two + sign)).start()
            def forward_all(place, _):
                forward(place)
                return 0

            lax.fori_loop(0, n, forward_all, 0)
            for side, sign in sides:
                source = (two - 2 * sign + 2 * n) % n
                ref = line(gem, core, source)
                arrive(ref, ge_two.at[side])
                remote(ref, ref, ge_fwd.at[0, side], ge_third.at[side], second(two + sign)).start()
                ref = line(gem, core, source, side)
                remote(ref, ref, ge_fwd.at[1, side], ge_four.at[side], second(two + 2 * sign)).start()
            hand_over(two)
            keep_own()
            for side, sign in sides:
                source = (two - sign + n) % n
                arrive(line(gkv, core, source), gb_near.at[side])
                arrive(line(gem, core, source), ge_near.at[side])
                hand_over(source)
            for side, sign in sides:
                hand_over((two - 2 * sign + 2 * n) % n)
            last = (two + 4) % n
            for kind in range(2):
                ref = results[kind][1]
                third, four = ((gb_third, gb_four), (ge_third, ge_four))[kind]
                for side, sign in sides:
                    source = (two - 3 * sign + 3 * n) % n
                    arrive(line(ref, core, source), third.at[side])
                    hand_over(source, results[kind:kind + 1])
                for side in range(2):
                    arrive(line(ref, core, last, side), four.at[side])
                hand_over(last, results[kind:kind + 1])

            def take(place, _):
                for kind, ref in results:
                    theirs = line(ref, 1 - core, place)
                    arrive(theirs, gc_recv.at[kind, place])
                return 0

            lax.fori_loop(0, n, take, 0)

            def sent_lines(place, _):
                for kind, ref in results:
                    mine = line(ref, core, place)
                    remote(mine, mine, gc_send.at[kind, place], gc_recv.at[kind, place], partner).wait_send()
                return 0

            lax.fori_loop(0, n, sent_lines, 0)
            for side in range(2):
                for i in range(2):
                    for ref, sends in ((gkv, gb_send), (gem, ge_send)):
                        mine = line(ref, core, two)
                        remote(mine, mine, sends.at[i, side], g_sem.at[1], partner).wait_send()
                for ref, sends in ((gkv, gb_fwd), (gem, ge_fwd)):
                    mine = line(ref, core, two)
                    remote(mine, mine, sends.at[0, side], g_sem.at[1], partner).wait_send()
                    mine = line(ref, core, two, side)
                    remote(mine, mine, sends.at[1, side], g_sem.at[1], partner).wait_send()


def write_out(kv, em, *refs):
    states, (okv, oem), out_states, em_out, sem = refs[:4], refs[4:6], refs[6:10], refs[10], refs[11]
    writes = [pltpu.make_async_copy(kv, okv, sem.at[0])]
    writes += [pltpu.make_async_copy(states[i], out_states[i], sem.at[1 + i]) for i in range(4)]
    for copy in writes:
        copy.start()
    rows, width = em_out.shape
    cut = rows // 4
    for i in range(4):
        for row in range(i * cut, (i + 1) * cut, 8):
            em_out[row:row + 8, :] = em[row // 2:row // 2 + 4].reshape(8, width)
        writes.append(pltpu.make_async_copy(em_out.at[pl.ds(i * cut, cut)], oem.at[pl.ds(i * cut, cut)], sem.at[5 + i]))
        writes[-1].start()
    for copy in writes:
        copy.wait()


def solution(mesh):
    owners, blocks = mesh.shape["dp"], mesh.shape["mp"]
    n = math.isqrt(owners)

    def shards(kv_up_grads, tok_grads, token_rows, step_count, master, moment_one, moment_two, average):
        cols, width, tokens = kv_up_grads.shape[1], tok_grads.shape[1], tok_grads.shape[0]
        rows = master.shape[1] // LANES
        half, ehalf = cols // 2, width // 2
        lines = lambda array: array.reshape(rows, LANES)
        dma, f32, bf16 = pltpu.SemaphoreType.DMA, jnp.float32, jnp.bfloat16
        any_space = pl.BlockSpec(memory_space=pltpu.HBM)
        vmem = pl.BlockSpec(memory_space=pltpu.VMEM)
        stay = lambda array: pltpu.with_memory_space_constraint(array, pltpu.HBM)
        state = jax.ShapeDtypeStruct((rows, LANES), f32)
        share = half // LANES + 2

        def body(*refs):
            step_kernel(n, blocks, cols, width, *refs)

        outs = pl.pallas_call(
            body,
            out_shape=(
                jax.ShapeDtypeStruct((n, n, ROWS, cols), bf16),
                jax.ShapeDtypeStruct((n, n, 2, width), bf16),
                state, state, state, state,
            ),
            in_specs=[any_space] * 3 + [pl.BlockSpec(memory_space=pltpu.SMEM)] + [any_space] * 4,
            out_specs=[vmem] * 6,
            scratch_shapes=[
                pltpu.VMEM((2, 3, n, ROWS, half), bf16),
                pltpu.VMEM((2, 2, 2, n, ROWS, half), bf16),
                pltpu.VMEM((2, 2, n // 2, ROWS, half), bf16),
                pltpu.VMEM((2, n, ROWS, half), f32),
                pltpu.VMEM((2, n, ROWS, half), f32),
                pltpu.VMEM((2, tokens, ehalf), bf16),
                pltpu.VMEM((2, 1, tokens), jnp.int32),
                pltpu.VMEM((n, 2 * n, ehalf), f32),
                pltpu.VMEM((2, 2 * n, ehalf), f32),
                pltpu.VMEM((2, 2 * n, ehalf), f32),
                pltpu.VMEM((2, n, ehalf), f32),
                pltpu.VMEM((2, 2 * n, ehalf), f32),
                pltpu.VMEM((2, 2 * n, ehalf), f32),
                pltpu.VMEM((share, n * ROWS, LANES), f32),
                pltpu.VMEM((n, share, ROWS, LANES), f32),
                pltpu.VMEM((2, share, ROWS, LANES), f32),
                pltpu.VMEM((4, rows, LANES), f32),
                pltpu.VMEM((n, 3, share, ROWS, LANES), f32),
                pltpu.VMEM((n, share, ROWS, LANES), f32),
                pltpu.VMEM((n, 1, LANES), f32),
                pltpu.VMEM((n, 1, LANES), f32),
                pltpu.VMEM((2, blocks, 1, LANES), f32),
                pltpu.VMEM((2 * (ehalf // LANES), LANES), f32),
                dma((4,)), dma((6,)),
                dma((3, 6)), dma((2, 3)), dma((2, 2, 2)), dma((2, 2)), dma((2,)), dma((2,)),
                dma((3, 2)), dma((2,)), dma((2,)), dma((2,)), dma((2,)), dma((2,)),
                dma((2, n)), dma((2, n)), dma((2,)),
                dma((n,)), dma((n,)), dma((n,)), dma((n,)),
                dma((2 * blocks,)), dma((2, blocks)),
                dma((3, n)), dma((3, n)), dma((n,)), dma((n,)),
                dma((2, 2)), dma((2,)), dma((2, n)), dma((2, 2)), dma((2,)), dma((2,)),
                dma((2, 2)), dma((2,)), dma((2,)), dma((2, 2)), dma((2,)), dma((2,)),
                dma((2, n)), dma((2, n)), pltpu.SemaphoreType.REGULAR,
            ],
            compiler_params=pltpu.CompilerParams(
                collective_id=0, has_side_effects=True, vmem_limit_bytes=48 * 1024 * 1024
            ),
            name="adam_step",
        )(
            stay(kv_up_grads.reshape(n, n, ROWS, cols)), stay(tok_grads), stay(token_rows.reshape(1, tokens)), step_count,
            stay(lines(master)), stay(lines(moment_one)), stay(lines(moment_two)), stay(lines(average)),
        )
        new_kv_up, new_embed, *states = outs
        new_kv_up, new_embed, *states = pl.pallas_call(
            write_out,
            out_shape=(
                jax.ShapeDtypeStruct(new_kv_up.shape, bf16), jax.ShapeDtypeStruct((owners * 2, width), bf16),
                state, state, state, state,
            ),
            in_specs=[vmem] * 6,
            out_specs=[any_space] * 6,
            scratch_shapes=[pltpu.VMEM((owners * 2, width), bf16), dma((9,))],
            compiler_params=pltpu.CompilerParams(vmem_limit_bytes=16 * 1024 * 1024),
            name="write_out",
        )(new_kv_up, new_embed.reshape(owners, 2, width), *states)
        return (
            new_kv_up.reshape(owners * ROWS, cols),
            new_embed,
            *[array.reshape(1, rows * LANES) for array in states],
        )

    placed = (
        P(("group", "dp"), "mp"),
        P(("group", "dp"), None),
        P(("group", "dp")),
        P(),
        P("mp", "dp"),
        P("mp", "dp"),
        P("mp", "dp"),
        P("mp", "dp"),
    )
    return jax.shard_map(
        shards,
        mesh=mesh,
        in_specs=placed,
        out_specs=(
            P(None, "mp"),
            P("mp", None),
            P("mp", "dp"),
            P("mp", "dp"),
            P("mp", "dp"),
            P("mp", "dp"),
        ),
        check_vma=False,
    )
```
